128 devices in a mesh: leaf: 16 (over x_lo, y, core), grid: 8 (over x_hi, z).
Axes of the slice: x: 4 (x_hi: 2, x_lo: 2; x = x_hi * 2 + x_lo), y: 4, z: 4, core: 2. Of those that a mesh axis runs over, the one named last changes fastest.
Arguments:
- child_front: float32 [16, 1, 2048, 2, 8, 128], P('leaf', None, None, None, 'grid'), as said below
- child_live: int32 [16, 1, 16], replicated, may hold values 0 or 1
- child_map: int32 [16, 1, 8], replicated, may hold values from 0 to 15, as said below
- parent_owner: int32 [8, 16], replicated, may hold values from 0 to 15, as said below
- parent_shift: float32 [16, 1, 1, 8, 128], P('leaf', None, None, 'grid'), may hold values from 0.5 to 2
Outputs:
- child_factor: float32 [16, 1, 2048, 1, 8, 128], P('leaf', None, None, None, 'grid')
- parent_done: float32 [16, 1, 2048, 1, 8, 128], P('leaf', None, None, None, 'grid')
The draws below stay inside these ranges and needn't reach their ends.
Inputs may be any that keep to these rules, and one draw needn't show every extreme that they name: `child_map`: each row holds 8 different block numbers in increasing order, the last one being 15. `parent_owner`: each row is a permutation of the 16 slots. `child_front`: each front is symmetric positive definite.
All inputs are finite; a program needn't handle non-finite values.
Results may differ from the reference program's by a relative error of at most 0.0003.
Values sent between devices are 32-bit elements; how exact they have to be, the bound alone decides.
No kernel may reach another device: no remote copies, remote signals or barrier semaphores. Data moves between devices by JAX's collectives and lax.ppermute only.
A program may use at most 128 MiB of HBM per device.

```python
import math
import jax
import jax.numpy as jnp
from jax import lax

F = 2048
PIVOTS = 1024
NB = 128
FRONTS_DEV = 1
FB = 16
PB = 8
CB = 8
POS = 16
PAIRS = 8
T1 = 2
TP = 1
T2 = 1
N_GRID = 8


def draw_child_front(key, part):
    count = POS * FRONTS_DEV
    factor = jax.random.normal(jax.random.fold_in(key, 11), (count, F, F), jnp.float32)
    gram = jnp.einsum('pik,pjk->pij', factor, factor, precision=lax.Precision.HIGHEST) / F
    gram = 0.5 * (gram + jnp.swapaxes(gram, 1, 2))
    shift = jax.random.uniform(jax.random.fold_in(key, 13), (count, F), jnp.float32, 0.5, 1.5)
    matrix = gram + shift[:, :, None] * jnp.eye(F, dtype=jnp.float32)[None]
    return matrix.reshape(POS, FRONTS_DEV, F, T1, F // (NB * T1), NB)


def draw_child_map(key, part):
    count = POS * FRONTS_DEV
    keys = jax.random.split(jax.random.fold_in(key, 21), count)
    orders = jax.vmap(lambda single: jax.random.permutation(single, FB - 1))(keys)
    chosen = jnp.sort(orders[:, :CB - 1].astype(jnp.int32), axis=1)
    closing = jnp.full((count, 1), FB - 1, jnp.int32)
    return jnp.concatenate([chosen, closing], axis=1).reshape(POS, FRONTS_DEV, CB)


def draw_parent_owner(key, part):
    keys = jax.random.split(jax.random.fold_in(key, 31), PAIRS)
    return jax.vmap(lambda single: jax.random.permutation(single, FB))(keys).astype(jnp.int32)


def place_ends(values, key, low, largest):
    shape = values.shape
    spot = [jax.random.randint(jax.random.fold_in(key, axis), (), 0, shape[axis]) for axis in range(len(shape))]
    values = values.at[tuple(spot)].set(low)
    longest = shape.index(max(shape))
    spot[longest] = (spot[longest] + 1) % shape[longest]
    return values.at[tuple(spot)].set(largest)


def level_of(stream_key, extent, cuts, least, top_value):
    def one(dim, parts):
        steps = jax.random.uniform(jax.random.fold_in(jax.random.fold_in(stream_key, 6), dim), (parts,), jnp.float32, least / len(cuts), top_value / len(cuts))
        return jnp.repeat(jnp.exp(steps), extent[dim] // parts).reshape((-1,) + (1,) * (len(extent) - dim - 1))

    loudness = one(*cuts[0])
    for cut in cuts[1:]:
        loudness = loudness * one(*cut)
    return loudness


def setup_inputs(seed: int = 0) -> dict:
    seeds = jax.random.split(jax.random.key(seed), 6)
    return {
        "child_front": draw_child_front(jax.random.fold_in(seeds[5], 71), 0),
        "child_live": place_ends((jax.random.randint(seeds[1], (POS, FRONTS_DEV, FB), 0, 4) < 3).astype(jnp.int32), jax.random.fold_in(seeds[1], 1), 0, 1),
        "child_map": draw_child_map(jax.random.fold_in(seeds[5], 71), 0),
        "parent_owner": draw_parent_owner(jax.random.fold_in(seeds[5], 71), 0),
        "parent_shift": jnp.clip(jnp.exp(math.log(2.0) - 1.3862944 * jax.random.uniform(seeds[4], (POS, FRONTS_DEV, T2, N_GRID, NB), jnp.float32) ** level_of(seeds[4], (POS, FRONTS_DEV, T2, N_GRID, NB), ((0, 16), (3, 8)), -0.2, 0.2)), 0.5, 2.0),
    }


highest = lax.Precision.HIGHEST

def partial_factor(matrix):
    lower_part = jnp.linalg.cholesky(matrix[:PIVOTS, :PIVOTS])
    below_part = lax.linalg.triangular_solve(lower_part, matrix[PIVOTS:, :PIVOTS], left_side=False, lower=True, transpose_a=True)
    schur = matrix[PIVOTS:, PIVOTS:] - jnp.dot(below_part, below_part.T, precision=highest)
    return (jnp.concatenate([lower_part, below_part], axis=0), schur)

def assemble_child(entries, alive):
    matrix = entries.reshape(F, F)
    live_rows = jnp.repeat(alive.astype(jnp.float32), NB)
    identity = jnp.eye(F, dtype=jnp.float32)
    return matrix * live_rows[:, None] * live_rows[None, :] + identity * (1.0 - live_rows)[:, None]

def extend_schur(schur, targets, alive):
    place = (targets[None, :] == jnp.arange(FB, dtype=jnp.int32)[:, None]).astype(jnp.float32)
    place = place * alive.astype(jnp.float32)[None, :]
    tiles = schur.reshape(CB, NB, CB, NB)
    rows_done = jnp.einsum('bc,cidj->bidj', place, tiles, precision=highest)
    both_done = jnp.einsum('bidj,ed->bie j'.replace(' ', ''), rows_done, place, precision=highest)
    return both_done.reshape(F, F)

def reference(child_front, child_live, child_map, parent_owner, parent_shift):
    grid_count = F // (NB * T1)
    child_rows = []
    schurs = []
    for position in range(POS):
        factor_row = []
        schur_row = []
        for front_id in range(FRONTS_DEV):
            matrix = assemble_child(child_front[position, front_id], child_live[position, front_id])
            factor, schur = partial_factor(matrix)
            factor_row.append(factor.reshape(F, TP, grid_count, NB))
            schur_row.append(schur)
        child_rows.append(jnp.stack(factor_row))
        schurs.append(schur_row)
    child_factor = jnp.stack(child_rows)
    parent_rows = [[None] * FRONTS_DEV for position in range(POS)]
    for pair in range(PAIRS):
        owner = parent_owner[pair]
        for front_id in range(FRONTS_DEV):
            slot_shift = jnp.stack([parent_shift[2 * pair + member, front_id] for member in range(2)])
            slot_shift = jnp.transpose(slot_shift, (0, 2, 1, 3)).reshape(FB, NB)
            matrix = jnp.diag(slot_shift[owner].reshape(F))
            for member in range(2):
                child = 2 * pair + member
                matrix = matrix + extend_schur(schurs[child][front_id], child_map[child, front_id], child_live[child, front_id, PB:])
            factor, schur = partial_factor(matrix)
            finished = jnp.zeros((F, F), jnp.float32).at[:, :PIVOTS].set(factor).at[PIVOTS:, PIVOTS:].set(schur)
            slots = jnp.zeros((F, FB, NB), jnp.float32).at[:, owner, :].set(finished.reshape(F, FB, NB))
            slots = jnp.transpose(slots.reshape(F, 2, grid_count, T2, NB), (1, 0, 3, 2, 4))
            for member in range(2):
                parent_rows[2 * pair + member][front_id] = slots[member]
    parent_done = jnp.stack([jnp.stack(row) for row in parent_rows])
    return (child_factor, parent_done)
```

```python
import functools

import jax
import jax.numpy as jnp
from jax import lax
from jax.experimental import pallas as pl
from jax.experimental.pallas import tpu as pltpu
from jax.sharding import PartitionSpec as P

NB = 128
PB = 8
FB = 16
HALF = PB * NB
F = FB * NB
VLIMIT = 56 << 20
f32 = jnp.float32
bf16 = jnp.bfloat16


def iota(shape, axis):
    return lax.broadcasted_iota(jnp.int32, shape, axis)


def split(x):
    high = x.astype(bf16)
    return high, (x - high.astype(f32)).astype(bf16)


def dot_nt(a, b):
    return lax.dot_general(a, b, (((1,), (1,)), ((), ())), preferred_element_type=f32)


def dot3(ah, al, bh, bl):
    return dot_nt(ah, bh) + (dot_nt(ah, bl) + dot_nt(al, bh))


def inverse_factor(block, width):
    groups = [block[8 * i : 8 * i + 8, :] for i in range(16)]
    lane = iota((8, NB), 1)
    sub = iota((8, NB), 0)
    own = width // 8
    for step in range(NB // width):
        first = width * step
        top = first // 8
        inside = (lane >= first) & (lane < first + width)
        spread = {}
        for i in range(top, 16):
            for j in range(width):
                if i < top + own and 8 * (i - top) + 7 < j:
                    continue
                spread[i, j] = jnp.broadcast_to(
                    groups[i][:, first + j : first + j + 1], (8, NB)
                )
        diag = {}
        for a in range(width):
            for b in range(a + 1):
                diag[a, b] = jnp.broadcast_to(
                    spread[top + a // 8, b][a % 8 : a % 8 + 1, :], (8, NB)
                )
        rows = []
        for a in range(width):
            row = jnp.broadcast_to(groups[top + a // 8][a % 8 : a % 8 + 1, :], (8, NB))
            rows.append(jnp.where(lane == first + a, 1.0, jnp.where(inside, 0.0, row)))
        recip = {}
        mult = {}
        for j in range(width):
            recip[j] = 1.0 / diag[j, j]
            for a in range(j + 1, width):
                mult[a, j] = diag[a, j] * recip[j]
            for b in range(j + 1, width):
                for a in range(b, width):
                    diag[a, b] = diag[a, b] - mult[a, j] * diag[b, j]
        solved = []
        for a in range(width):
            row = rows[a]
            for b in range(a):
                row = row - mult[a, b] * solved[b]
            solved.append(row)
        for q in range(own):
            total = None
            for s in range(8):
                a = 8 * q + s
                value = solved[a] * lax.rsqrt(diag[a, a])
                total = value if total is None else jnp.where(sub == s, value, total)
            groups[top + q] = total
        back = [None] * width
        for a in reversed(range(width)):
            row = solved[a] * recip[a]
            for b in range(a + 1, width):
                row = row - mult[b, a] * back[b]
            back[a] = row
        for i in range(top + own, 16):
            row = jnp.where(inside, 0.0, groups[i])
            for b in range(width):
                row = row - spread[i, b] * back[b]
            groups[i] = row
    return groups


def factor_chain(m, lh, ll, xh, xl, blocks):
    lower = iota((NB, NB), 0) >= iota((NB, NB), 1)

    def panel(k):
        lo = k * NB
        xhk = xh[k]
        xlk = xl[k]
        for r in range(k, blocks):
            rows = slice(r * NB, r * NB + NB)
            ch, cl = split(m[rows, lo : lo + NB])
            part = dot3(ch, cl, xhk, xlk)
            if r == k:
                part = jnp.where(lower, part, 0.0)
            m[rows, lo : lo + NB] = part
            ph, plow = split(part)
            lh[rows, lo : lo + NB] = ph
            ll[rows, lo : lo + NB] = plow
        if k + 1 < PB:
            nxt = lo + NB
            bh = lh[nxt : nxt + NB, :nxt]
            bl = ll[nxt : nxt + NB, :nxt]
            for r in range(k + 1, blocks, 2):
                rows = slice(r * NB, min(r + 2, blocks) * NB)
                change = dot3(lh[rows, :nxt], ll[rows, :nxt], bh, bl)
                m[rows, nxt : nxt + NB] = m[rows, nxt : nxt + NB] - change

    def body(k, carry):
        off = pl.multiple_of(k * NB, NB)
        groups = inverse_factor(m[pl.ds(off, NB), pl.ds(off, NB)], 16)
        for i in range(16):
            lane = iota((8, NB), 1)
            sub = iota((8, NB), 0) + 8 * i
            high, low = split(jnp.where(lane <= sub, groups[i], 0.0))
            xh[k, 8 * i : 8 * i + 8, :] = high
            xl[k, 8 * i : 8 * i + 8, :] = low
        for static in range(PB):
            pl.when(k == static)(functools.partial(panel, static))
        return carry

    lax.fori_loop(0, PB, body, 0)


def prepare_kernel(meta, front, shift, first_out, second_out):
    g = meta[0]
    eye = (iota((NB, NB), 0) == iota((NB, NB), 1)).astype(f32)

    def alive(block):
        return meta[2 + block].astype(f32)

    def sym(out, base, col, start):
        here = alive(start + g)
        for s in range(5):
            r = (g + s) % PB
            off = pl.multiple_of((start + r) * NB, NB)
            block = front[pl.ds(off, NB), col * NB : col * NB + NB]
            block = block * (here * alive(start + r))
            if s == 0:
                block = block + eye * (1.0 - here)

            @pl.when(r >= g)
            def _():
                out[base + s * NB : base + s * NB + NB, :] = block

            @pl.when(r < g)
            def _():
                out[base + s * NB : base + s * NB + NB, :] = block.T

    sym(first_out, 0, 0, 0)
    first_out[5 * NB : 5 * NB + 8, :] = jnp.broadcast_to(shift[0:1, :], (8, NB))
    here = alive(g)
    for r in range(PB):
        rows = slice(HALF + r * NB, HALF + r * NB + NB)
        second_out[r * NB : r * NB + NB, :] = front[rows, :NB] * (here * alive(PB + r))
    sym(second_out, HALF, 1, PB)


def place_sym(meta, parts, base, target):
    g = meta[0]
    for k in range(PB):
        h = g ^ k
        for s in range(5):
            r = (h + s) % PB
            row = pl.multiple_of(jnp.maximum(r, h) * NB, NB)
            col = pl.multiple_of(jnp.minimum(r, h) * NB, NB)
            target[pl.ds(row, NB), pl.ds(col, NB)] = parts[k][
                base + s * NB : base + s * NB + NB, :
            ]


def child_first_kernel(meta, *refs):
    parts = refs[:PB]
    lh, ll, xh, xl, column, shifts, m = refs[PB:]
    g = meta[0]
    place_sym(meta, parts, 0, m)
    shifts[...] = jnp.zeros_like(shifts)
    for k in range(PB):
        off = pl.multiple_of((g ^ k) * NB, NB)
        shifts[:, pl.ds(off, NB)] = parts[k][5 * NB : 5 * NB + 8, :]
    lh[...] = jnp.zeros_like(lh)
    ll[...] = jnp.zeros_like(ll)
    factor_chain(m, lh, ll, xh, xl, PB)
    mine = pl.multiple_of(g * NB, NB)
    for r in range(PB):
        block = m[r * NB : r * NB + NB, pl.ds(mine, NB)]
        column[r * NB : r * NB + NB, :] = jnp.where(r >= g, block, 0.0)


def child_second_kernel(meta, lh, ll, xh, xl, column, shifts, *refs):
    parts = refs[:PB]
    factor, schur, m, bh, bl = refs[PB:]
    g = meta[0]
    for k in range(PB):
        off = pl.multiple_of((g ^ k) * NB, NB)
        m[:, pl.ds(off, NB)] = parts[k][:HALF, :]
    place_sym(meta, parts, HALF, schur)
    schur[HALF : HALF + 8, :] = shifts[...]
    for k in range(PB):
        lo = k * NB
        for r in range(0, PB, 2):
            rows = slice(r * NB, r * NB + 2 * NB)
            value = m[rows, lo : lo + NB]
            if k:
                value = value - dot3(
                    bh[rows, :lo], bl[rows, :lo], lh[lo : lo + NB, :lo], ll[lo : lo + NB, :lo]
                )
            ch, cl = split(value)
            part = dot3(ch, cl, xh[k], xl[k])
            m[rows, lo : lo + NB] = part
            ph, plow = split(part)
            bh[rows, lo : lo + NB] = ph
            bl[rows, lo : lo + NB] = plow
    lower = iota((NB, NB), 0) >= iota((NB, NB), 1)
    for c in range(0, PB, 2):
        cols = slice(c * NB, c * NB + 2 * NB)
        for r in range(c, PB, 2):
            rows = slice(r * NB, r * NB + 2 * NB)
            change = dot3(bh[rows, :], bl[rows, :], bh[cols, :], bl[cols, :])
            schur[rows, cols] = schur[rows, cols] - change
    mine = pl.multiple_of(g * NB, NB)
    factor[:HALF, :] = column[...]
    factor[HALF:, :] = m[:, pl.ds(mine, NB)]


def parent_kernel(meta, own, other, out, m, lh, ll, xh, xl, inverse):
    g = meta[0]
    member = meta[1]
    slot = member * PB + g
    for side in range(2):
        for q in range(FB):
            inverse[side, q] = -1
        for c in range(PB):
            live = meta[2 + 16 * side + PB + c]
            dest = meta[34 + 8 * side + c]
            inverse[side, dest] = jnp.where(live > 0, c, -1)
    mine = jnp.int32(0)
    for q in range(FB):
        mine = jnp.where(meta[50 + q] == slot, q, mine)
    sides = (own, other)
    eye = iota((NB, NB), 0) == iota((NB, NB), 1)

    def diagonal(block):
        holder = meta[50 + block]
        off = pl.multiple_of(holder % PB * NB, NB)
        a = own[HALF : HALF + 1, pl.ds(off, NB)]
        b = other[HALF : HALF + 1, pl.ds(off, NB)]
        row = jnp.where(holder // PB == member, a, b)
        return jnp.where(eye, jnp.broadcast_to(row, (NB, NB)), 0.0)

    for p in range(PB):
        for q in range(p, FB):
            where = (slice(q * NB, q * NB + NB), slice(p * NB, p * NB + NB))
            m[where] = diagonal(p) if p == q else jnp.zeros((NB, NB), f32)
            for side in range(2):
                ci = inverse[side, q]
                cj = inverse[side, p]

                @pl.when((ci >= 0) & (cj >= 0))
                def _():
                    ro = pl.multiple_of(ci * NB, NB)
                    co = pl.multiple_of(cj * NB, NB)
                    m[where] = m[where] + sides[side][pl.ds(ro, NB), pl.ds(co, NB)]

    lh[...] = jnp.zeros_like(lh)
    ll[...] = jnp.zeros_like(ll)
    factor_chain(m, lh, ll, xh, xl, FB)

    @pl.when(mine < PB)
    def _():
        off = pl.multiple_of(mine * NB, NB)
        for r in range(FB):
            block = m[r * NB : r * NB + NB, pl.ds(off, NB)]
            out[r * NB : r * NB + NB, :] = jnp.where(r >= mine, block, 0.0)

    @pl.when(mine >= PB)
    def _():
        out[:HALF, :] = jnp.zeros((HALF, NB), f32)
        off = pl.multiple_of(mine * NB, NB)
        rh = lh[pl.ds(off, NB), :]
        rl = ll[pl.ds(off, NB), :]
        diag = diagonal(mine)
        for q in range(PB, FB):
            rows = slice(q * NB, q * NB + NB)
            out[rows, :] = jnp.where(mine == q, diag, 0.0) - dot3(
                lh[rows, :], ll[rows, :], rh, rl
            )
            for side in range(2):
                ci = inverse[side, q]
                cj = inverse[side, mine]
                high = pl.multiple_of(jnp.maximum(jnp.maximum(ci, cj), 0) * NB, NB)
                low = pl.multiple_of(jnp.maximum(jnp.minimum(ci, cj), 0) * NB, NB)

                @pl.when((ci >= cj) & (cj >= 0))
                def _():
                    out[rows, :] = out[rows, :] + sides[side][pl.ds(high, NB), pl.ds(low, NB)]

                @pl.when((ci >= 0) & (ci < cj))
                def _():
                    out[rows, :] = out[rows, :] + sides[side][pl.ds(high, NB), pl.ds(low, NB)].T


VM = pl.BlockSpec(memory_space=pltpu.VMEM)
SM = pl.BlockSpec(memory_space=pltpu.SMEM)


def shape(*dims, dtype=f32):
    return jax.ShapeDtypeStruct(dims, dtype)


def run(kernel, outs, scratch, flops, meta, *args):
    return pl.pallas_call(
        kernel,
        out_shape=outs,
        in_specs=[SM] + [VM] * len(args),
        out_specs=jax.tree.map(lambda _: VM, outs),
        scratch_shapes=scratch,
        compiler_params=pltpu.CompilerParams(vmem_limit_bytes=VLIMIT),
        cost_estimate=pl.CostEstimate(flops=flops, bytes_accessed=1 << 22, transcendentals=0),
    )(meta, *args)


def exchange(value):
    parts = [value]
    for k in range(1, PB):
        parts.append(lax.ppermute(value, "grid", [(s, s ^ k) for s in range(PB)]))
    return parts


def body(child_front, child_live, child_map, parent_owner, parent_shift):
    g = lax.axis_index("grid").astype(jnp.int32)
    leaf = lax.axis_index("leaf").astype(jnp.int32)
    sibling = leaf ^ 1

    def row(table, index):
        return lax.dynamic_index_in_dim(table.reshape(table.shape[0], -1), index, 0, keepdims=False)

    meta = jnp.concatenate(
        [
            jnp.stack([g, leaf % 2]),
            row(child_live, leaf),
            row(child_live, sibling),
            row(child_map, leaf),
            row(child_map, sibling),
            row(parent_owner, leaf // 2),
        ]
    )
    front = child_front.reshape(F, 2 * NB)
    shift = parent_shift.reshape(1, NB)
    first, second = run(
        prepare_kernel,
        (shape(5 * NB + 8, NB), shape(HALF + 5 * NB, NB)),
        [],
        1 << 20,
        meta,
        front,
        shift,
    )
    first_parts = exchange(first)
    first_parts, second = lax.optimization_barrier((first_parts, second))
    second_parts = exchange(second)
    square = shape(HALF, HALF, dtype=bf16)
    lh, ll, xh, xl, column, shifts = run(
        child_first_kernel,
        (
            square,
            square,
            shape(PB, NB, NB, dtype=bf16),
            shape(PB, NB, NB, dtype=bf16),
            shape(HALF, NB),
            shape(8, HALF),
        ),
        [pltpu.VMEM((HALF, HALF), f32)],
        40 * 10**9,
        meta,
        *first_parts,
    )
    factor, schur = run(
        child_second_kernel,
        (shape(F, NB), shape(HALF + 8, HALF)),
        [
            pltpu.VMEM((HALF, HALF), f32),
            pltpu.VMEM((HALF, HALF), bf16),
            pltpu.VMEM((HALF, HALF), bf16),
        ],
        10**10,
        meta,
        lh,
        ll,
        xh,
        xl,
        column,
        shifts,
        *second_parts,
    )
    other = lax.ppermute(schur, "leaf", [(s, s ^ 1) for s in range(lax.axis_size("leaf"))])
    done = run(
        parent_kernel,
        shape(F, NB),
        [
            pltpu.VMEM((F, HALF), f32),
            pltpu.VMEM((F, HALF), bf16),
            pltpu.VMEM((F, HALF), bf16),
            pltpu.VMEM((PB, NB, NB), bf16),
            pltpu.VMEM((PB, NB, NB), bf16),
            pltpu.SMEM((2, FB), jnp.int32),
        ],
        40 * 10**9,
        meta,
        schur,
        other,
    )
    return factor.reshape(1, 1, F, 1, 1, NB), done.reshape(1, 1, F, 1, 1, NB)


def solution(mesh):
    in_specs = (
        P("leaf", None, None, None, "grid", None),
        P(),
        P(),
        P(),
        P("leaf", None, None, "grid", None),
    )
    out_specs = (
        P("leaf", None, None, None, "grid", None),
        P("leaf", None, None, None, "grid", None),
    )
    return jax.shard_map(body, mesh=mesh, in_specs=in_specs, out_specs=out_specs, check_vma=False)
```

```python
import functools

import jax
import jax.numpy as jnp
from jax import lax
from jax.experimental import pallas as pl
from jax.experimental.pallas import tpu as pltpu
from jax.sharding import PartitionSpec as P

NB = 128
PB = 8
FB = 16
HALF = PB * NB
QUART = HALF // 2
F = FB * NB
VLIMIT = 56 << 20
f32 = jnp.float32
bf16 = jnp.bfloat16


def iota(shape, axis):
    return lax.broadcasted_iota(jnp.int32, shape, axis)


def split(x):
    high = x.astype(bf16)
    return high, (x - high.astype(f32)).astype(bf16)


def dot_nt(a, b):
    return lax.dot_general(a, b, (((1,), (1,)), ((), ())), preferred_element_type=f32)


def dot3(ah, al, bh, bl):
    return dot_nt(ah, bh) + (dot_nt(ah, bl) + dot_nt(al, bh))


def inverse_factor(block, width):
    groups = [block[8 * i : 8 * i + 8, :] for i in range(16)]
    lane = iota((8, NB), 1)
    sub = iota((8, NB), 0)
    own = width // 8
    for step in range(NB // width):
        first = width * step
        top = first // 8
        inside = (lane >= first) & (lane < first + width)
        spread = {}
        for i in range(top, 16):
            for j in range(width):
                if i < top + own and 8 * (i - top) + 7 < j:
                    continue
                spread[i, j] = jnp.broadcast_to(
                    groups[i][:, first + j : first + j + 1], (8, NB)
                )
        diag = {}
        for a in range(width):
            for b in range(a + 1):
                diag[a, b] = jnp.broadcast_to(
                    spread[top + a // 8, b][a % 8 : a % 8 + 1, :], (8, NB)
                )
        rows = []
        for a in range(width):
            row = jnp.broadcast_to(groups[top + a // 8][a % 8 : a % 8 + 1, :], (8, NB))
            rows.append(jnp.where(lane == first + a, 1.0, jnp.where(inside, 0.0, row)))
        recip = {}
        mult = {}
        for j in range(width):
            recip[j] = 1.0 / diag[j, j]
            for a in range(j + 1, width):
                mult[a, j] = diag[a, j] * recip[j]
            for b in range(j + 1, width):
                for a in range(b, width):
                    diag[a, b] = diag[a, b] - mult[a, j] * diag[b, j]
        solved = []
        for a in range(width):
            row = rows[a]
            for b in range(a):
                row = row - mult[a, b] * solved[b]
            solved.append(row)
        for q in range(own):
            total = None
            for s in range(8):
                a = 8 * q + s
                value = solved[a] * lax.rsqrt(diag[a, a])
                total = value if total is None else jnp.where(sub == s, value, total)
            groups[top + q] = total
        back = [None] * width
        for a in reversed(range(width)):
            row = solved[a] * recip[a]
            for b in range(a + 1, width):
                row = row - mult[b, a] * back[b]
            back[a] = row
        for i in range(top + own, 16):
            row = jnp.where(inside, 0.0, groups[i])
            for b in range(width):
                row = row - spread[i, b] * back[b]
            groups[i] = row
    return groups


def dot3_cat(ah, al, both):
    wide = dot_nt(ah, both)
    return wide[:, :NB] + (wide[:, NB:] + dot_nt(al, both[:NB, :]))


def factor_half(m, lh, ll, xcat, start, origin, blocks, active):
    lower = iota((NB, NB), 0) >= iota((NB, NB), 1)
    eye = iota((NB, NB), 0) == iota((NB, NB), 1)
    base = start * NB

    def solve(k, r, count):
        lo = k * NB
        rows = slice(r * NB, (r + count) * NB)
        ch, cl = split(m[rows, lo : lo + NB])
        part = dot3_cat(ch, cl, xcat[origin + k - start])
        if r == k:
            part = jnp.where(lower, part, 0.0)
        m[rows, lo : lo + NB] = part
        ph, plow = split(part)
        lh[rows, lo : lo + NB] = ph
        ll[rows, lo : lo + NB] = plow

    def panel(k):
        solve(k, k, 1)

        @pl.when(active(k))
        def _():
            for r in range(k + 1, blocks, 2):
                solve(k, r, min(2, blocks - r))

        if k + 1 < start + 4:
            nxt = k * NB + NB
            cols = slice(base, nxt)
            both = jnp.concatenate([lh[nxt : nxt + NB, cols], ll[nxt : nxt + NB, cols]], axis=0)
            for r in range(k + 1, blocks, 2):
                rows = slice(r * NB, min(r + 2, blocks) * NB)
                change = dot3_cat(lh[rows, cols], ll[rows, cols], both)
                m[rows, nxt : nxt + NB] = m[rows, nxt : nxt + NB] - change

    def store(k, i, value):
        high, low = split(value)
        count = value.shape[0]
        xcat[origin + k, 8 * i : 8 * i + count, :] = high
        xcat[origin + k, NB + 8 * i : NB + 8 * i + count, :] = low

    def body(k, carry):
        off = pl.multiple_of(base + k * NB, NB)
        busy = active(start + k)

        @pl.when(busy)
        def _():
            groups = inverse_factor(m[pl.ds(off, NB), pl.ds(off, NB)], 16)
            lane = iota((8, NB), 1)
            for i in range(16):
                sub = iota((8, NB), 0) + 8 * i
                store(k, i, jnp.where(lane <= sub, groups[i], 0.0))

        @pl.when(jnp.logical_not(busy))
        def _():
            store(k, 0, jnp.where(eye, lax.rsqrt(m[pl.ds(off, NB), pl.ds(off, NB)]), 0.0))

        for static in range(4):
            pl.when(k == static)(functools.partial(panel, start + static))
        return carry

    lax.fori_loop(0, 4, body, 0)


def subtract_square(m, lh, ll, row0, rows, col0, cols, left):
    wide = 2 * NB
    for c in range(col0, col0 + cols, wide):
        for r in range(max(row0, c), row0 + rows, wide):
            change = dot3(
                lh[r : r + wide, left], ll[r : r + wide, left], lh[c : c + wide, left], ll[c : c + wide, left]
            )
            m[r : r + wide, c : c + wide] = m[r : r + wide, c : c + wide] - change


def prepare_kernel(meta, front, shift, first_out, second_out):
    g = meta[0]
    eye = (iota((NB, NB), 0) == iota((NB, NB), 1)).astype(f32)

    def alive(block):
        return meta[2 + block].astype(f32)

    def sym(out, base, col, start):
        here = alive(start + g)
        for s in range(5):
            r = (g + s) % PB
            off = pl.multiple_of((start + r) * NB, NB)
            block = front[pl.ds(off, NB), col * NB : col * NB + NB]
            block = block * (here * alive(start + r))
            if s == 0:
                block = block + eye * (1.0 - here)

            @pl.when(r >= g)
            def _():
                out[base + s * NB : base + s * NB + NB, :] = block

            @pl.when(r < g)
            def _():
                out[base + s * NB : base + s * NB + NB, :] = block.T

    sym(first_out, 0, 0, 0)
    first_out[5 * NB : 5 * NB + 8, :] = jnp.broadcast_to(shift[0:1, :], (8, NB))
    here = alive(g)
    for r in range(PB):
        rows = slice(HALF + r * NB, HALF + r * NB + NB)
        second_out[r * NB : r * NB + NB, :] = front[rows, :NB] * (here * alive(PB + r))
    sym(second_out, HALF, 1, PB)


OFFSETS = ((0, 0), (0, 3), (0, 1), (0, 2), (1, 0), (1, 3), (1, 1), (1, 2))


def holder_of(meta, k):
    g = meta[0]
    dx, dz = OFFSETS[k]
    return (g // 4 ^ dx) * 4 + (g % 4 + dz) % 4


def place_sym(meta, parts, base, target):
    for k in range(PB):
        h = holder_of(meta, k)
        for s in range(5):
            r = (h + s) % PB
            row = pl.multiple_of(jnp.maximum(r, h) * NB, NB)
            col = pl.multiple_of(jnp.minimum(r, h) * NB, NB)
            target[pl.ds(row, NB), pl.ds(col, NB)] = parts[k][
                base + s * NB : base + s * NB + NB, :
            ]


def child_first_kernel(meta, *refs):
    parts = refs[:PB]
    lh, ll, xcat, column, shifts, rest, m = refs[PB:]
    g = meta[0]
    place_sym(meta, parts, 0, m)
    shifts[...] = jnp.zeros_like(shifts)
    for k in range(PB):
        off = pl.multiple_of(holder_of(meta, k) * NB, NB)
        shifts[:, pl.ds(off, NB)] = parts[k][5 * NB : 5 * NB + 8, :]
    rest[...] = m[QUART:, QUART:]
    lh[...] = jnp.zeros_like(lh)
    ll[...] = jnp.zeros_like(ll)
    factor_half(m, lh, ll, xcat, 0, 0, PB, lambda k: meta[2 + k] > 0)

    @pl.when(g < 4)
    def _():
        mine = pl.multiple_of(g * NB, NB)
        for r in range(PB):
            block = m[r * NB : r * NB + NB, pl.ds(mine, NB)]
            column[r * NB : r * NB + NB, :] = jnp.where(r >= g, block, 0.0)


def child_second_kernel(meta, rest, ah, al, lh, ll, xcat, column, m):
    g = meta[0]
    m[...] = rest[...]
    wide = 2 * NB
    for c in range(0, QUART, wide):
        for r in range(c, QUART, wide):
            change = dot3(
                ah[QUART + r : QUART + r + wide, :],
                al[QUART + r : QUART + r + wide, :],
                ah[QUART + c : QUART + c + wide, :],
                al[QUART + c : QUART + c + wide, :],
            )
            m[r : r + wide, c : c + wide] = m[r : r + wide, c : c + wide] - change
    lh[...] = jnp.zeros_like(lh)
    ll[...] = jnp.zeros_like(ll)
    factor_half(m, lh, ll, xcat, 0, 0, 4, lambda k: meta[6 + k] > 0)

    @pl.when(g >= 4)
    def _():
        mine = pl.multiple_of((g - 4) * NB, NB)
        for r in range(4):
            block = m[r * NB : r * NB + NB, pl.ds(mine, NB)]
            column[r * NB : r * NB + NB, :] = jnp.where(r >= g - 4, block, 0.0)


def solve_quarter(m, bh, bl, lh, ll, xcat, base):
    step = 2 * NB

    def block(k):
        lo = base + k * NB
        for r in range(0, HALF, step):
            ch, cl = split(m[r : r + step, lo : lo + NB])
            part = dot3_cat(ch, cl, xcat[k])
            m[r : r + step, lo : lo + NB] = part
            ph, plow = split(part)
            bh[r : r + step, lo : lo + NB] = ph
            bl[r : r + step, lo : lo + NB] = plow

    def update(first, count):
        left = slice(base + first * NB, base + (first + count) * NB)
        inner = slice(first * NB, (first + count) * NB)
        target = slice((first + count) * NB, (first + 2 * count) * NB)
        out = slice(base + target.start, base + target.stop)
        th = lh[target, inner]
        tl = ll[target, inner]
        for r in range(0, HALF, step):
            rows = slice(r, r + step)
            m[rows, out] = m[rows, out] - dot3(bh[rows, left], bl[rows, left], th, tl)

    block(0)
    update(0, 1)
    block(1)
    update(0, 2)
    block(2)
    update(2, 1)
    block(3)


def child_third_kernel(meta, ah, al, xa, ca, shifts, lh, ll, xb, cb, *refs):
    parts = refs[:PB]
    factor, schur, m, bh, bl = refs[PB:]
    g = meta[0]
    for k in range(PB):
        off = pl.multiple_of(holder_of(meta, k) * NB, NB)
        m[:, pl.ds(off, NB)] = parts[k][:HALF, :]
    place_sym(meta, parts, HALF, schur)
    schur[HALF : HALF + 8, :] = shifts[...]
    solve_quarter(m, bh, bl, ah, al, xa, 0)
    th = ah[QUART:, :]
    tl = al[QUART:, :]
    for r in range(0, HALF, 2 * NB):
        rows = slice(r, r + 2 * NB)
        m[rows, QUART:] = m[rows, QUART:] - dot3(bh[rows, :QUART], bl[rows, :QUART], th, tl)
    solve_quarter(m, bh, bl, lh, ll, xb, QUART)
    subtract_square(schur, bh, bl, 0, HALF, 0, HALF, slice(0, HALF))

    @pl.when(g < 4)
    def _():
        factor[:HALF, :] = ca[...]

    @pl.when(g >= 4)
    def _():
        factor[:QUART, :] = jnp.zeros((QUART, NB), f32)
        factor[QUART:HALF, :] = cb[...]

    factor[HALF:, :] = m[:, pl.ds(pl.multiple_of(g * NB, NB), NB)]


def parent_kernel(meta, own, other, out, m, lh, ll, xcat, inverse):
    g = meta[0]
    member = meta[1]
    slot = member * PB + g
    for side in range(2):
        for q in range(FB):
            inverse[side, q] = -1
        for c in range(PB):
            live = meta[2 + 16 * side + PB + c]
            dest = meta[34 + 8 * side + c]
            inverse[side, dest] = jnp.where(live > 0, c, -1)
    mine = jnp.int32(0)
    for q in range(FB):
        mine = jnp.where(meta[50 + q] == slot, q, mine)
    sides = (own, other)
    eye = iota((NB, NB), 0) == iota((NB, NB), 1)

    def diagonal(block):
        holder = meta[50 + block]
        off = pl.multiple_of(holder % PB * NB, NB)
        a = own[HALF : HALF + 1, pl.ds(off, NB)]
        b = other[HALF : HALF + 1, pl.ds(off, NB)]
        row = jnp.where(holder // PB == member, a, b)
        return jnp.where(eye, jnp.broadcast_to(row, (NB, NB)), 0.0)

    for p in range(PB):
        for q in range(p, FB):
            where = (slice(q * NB, q * NB + NB), slice(p * NB, p * NB + NB))
            m[where] = diagonal(p) if p == q else jnp.zeros((NB, NB), f32)
            for side in range(2):
                ci = inverse[side, q]
                cj = inverse[side, p]

                @pl.when((ci >= 0) & (cj >= 0))
                def _():
                    ro = pl.multiple_of(ci * NB, NB)
                    co = pl.multiple_of(cj * NB, NB)
                    m[where] = m[where] + sides[side][pl.ds(ro, NB), pl.ds(co, NB)]

    lh[...] = jnp.zeros_like(lh)
    ll[...] = jnp.zeros_like(ll)


    def touched(p):
        return (inverse[0, p] >= 0) | (inverse[1, p] >= 0)

    factor_half(m, lh, ll, xcat, 0, 0, FB, touched)
    subtract_square(m, lh, ll, QUART, F - QUART, QUART, QUART, slice(0, QUART))
    factor_half(m, lh, ll, xcat, 4, 4, FB, touched)

    @pl.when(mine < PB)
    def _():
        off = pl.multiple_of(mine * NB, NB)
        for r in range(FB):
            block = m[r * NB : r * NB + NB, pl.ds(off, NB)]
            out[r * NB : r * NB + NB, :] = jnp.where(r >= mine, block, 0.0)

    @pl.when(mine >= PB)
    def _():
        out[:HALF, :] = jnp.zeros((HALF, NB), f32)
        off = pl.multiple_of(mine * NB, NB)
        rh = lh[pl.ds(off, NB), :]
        rl = ll[pl.ds(off, NB), :]
        diag = diagonal(mine)
        for q in range(PB, FB):
            rows = slice(q * NB, q * NB + NB)
            out[rows, :] = jnp.where(mine == q, diag, 0.0) - dot3(
                lh[rows, :], ll[rows, :], rh, rl
            )
            for side in range(2):
                ci = inverse[side, q]
                cj = inverse[side, mine]
                high = pl.multiple_of(jnp.maximum(jnp.maximum(ci, cj), 0) * NB, NB)
                low = pl.multiple_of(jnp.maximum(jnp.minimum(ci, cj), 0) * NB, NB)

                @pl.when((ci >= cj) & (cj >= 0))
                def _():
                    out[rows, :] = out[rows, :] + sides[side][pl.ds(high, NB), pl.ds(low, NB)]

                @pl.when((ci >= 0) & (ci < cj))
                def _():
                    out[rows, :] = out[rows, :] + sides[side][pl.ds(high, NB), pl.ds(low, NB)].T


VM = pl.BlockSpec(memory_space=pltpu.VMEM)
SM = pl.BlockSpec(memory_space=pltpu.SMEM)


def shape(*dims, dtype=f32):
    return jax.ShapeDtypeStruct(dims, dtype)


def run(kernel, outs, scratch, flops, meta, *args):
    return pl.pallas_call(
        kernel,
        out_shape=outs,
        in_specs=[SM] + [VM] * len(args),
        out_specs=jax.tree.map(lambda _: VM, outs),
        scratch_shapes=scratch,
        compiler_params=pltpu.CompilerParams(vmem_limit_bytes=VLIMIT),
        cost_estimate=pl.CostEstimate(flops=flops, bytes_accessed=1 << 22, transcendentals=0),
    )(meta, *args)


def permute(value, dx, dz):
    pairs = [(x * 4 + z, (x ^ dx) * 4 + (z + dz) % 4) for x in range(2) for z in range(4)]
    return lax.ppermute(value, "grid", pairs)


def near(value):
    return [value] + [permute(value, 0, 1), permute(value, 0, 3), permute(value, 0, 2), permute(value, 1, 0)]


def far(parts):
    third, side = parts[3], parts[4]
    return parts + [permute(side, 0, 1), permute(side, 0, 3), permute(third, 1, 0)]


def body(child_front, child_live, child_map, parent_owner, parent_shift):
    g = lax.axis_index("grid").astype(jnp.int32)
    leaf = lax.axis_index("leaf").astype(jnp.int32)
    sibling = leaf ^ 1

    def row(table, index):
        return lax.dynamic_index_in_dim(table.reshape(table.shape[0], -1), index, 0, keepdims=False)

    meta = jnp.concatenate(
        [
            jnp.stack([g, leaf % 2]),
            row(child_live, leaf),
            row(child_live, sibling),
            row(child_map, leaf),
            row(child_map, sibling),
            row(parent_owner, leaf // 2),
        ]
    )
    front = child_front.reshape(F, 2 * NB)
    shift = parent_shift.reshape(1, NB)
    first, second = run(
        prepare_kernel,
        (shape(5 * NB + 8, NB), shape(HALF + 5 * NB, NB)),
        [],
        1 << 20,
        meta,
        front,
        shift,
    )
    first_parts = far(near(first))
    first_parts, second = lax.optimization_barrier((first_parts, second))
    second_near = near(second)
    ah, al, xa, ca, shifts, rest = run(
        child_first_kernel,
        (
            shape(HALF, QUART, dtype=bf16),
            shape(HALF, QUART, dtype=bf16),
            shape(4, 2 * NB, NB, dtype=bf16),
            shape(HALF, NB),
            shape(8, HALF),
            shape(QUART, QUART),
        ),
        [pltpu.VMEM((HALF, HALF), f32)],
        20 * 10**9,
        meta,
        *first_parts,
    )
    second_near, rest = lax.optimization_barrier((second_near, rest))
    second_parts = far(second_near)
    lh, ll, xb, cb = run(
        child_second_kernel,
        (
            shape(QUART, QUART, dtype=bf16),
            shape(QUART, QUART, dtype=bf16),
            shape(4, 2 * NB, NB, dtype=bf16),
            shape(QUART, NB),
        ),
        [pltpu.VMEM((QUART, QUART), f32)],
        20 * 10**9,
        meta,
        rest,
        ah,
        al,
    )
    factor, schur = run(
        child_third_kernel,
        (shape(F, NB), shape(HALF + 8, HALF)),
        [
            pltpu.VMEM((HALF, HALF), f32),
            pltpu.VMEM((HALF, HALF), bf16),
            pltpu.VMEM((HALF, HALF), bf16),
        ],
        10**10,
        meta,
        ah,
        al,
        xa,
        ca,
        shifts,
        lh,
        ll,
        xb,
        cb,
        *second_parts,
    )
    other = lax.ppermute(schur, "leaf", [(s, s ^ 1) for s in range(lax.axis_size("leaf"))])
    done = run(
        parent_kernel,
        shape(F, NB),
        [
            pltpu.VMEM((F, HALF), f32),
            pltpu.VMEM((F, HALF), bf16),
            pltpu.VMEM((F, HALF), bf16),
            pltpu.VMEM((PB, 2 * NB, NB), bf16),
            pltpu.SMEM((2, FB), jnp.int32),
        ],
        40 * 10**9,
        meta,
        schur,
        other,
    )
    return factor.reshape(1, 1, F, 1, 1, NB), done.reshape(1, 1, F, 1, 1, NB)


def solution(mesh):
    in_specs = (
        P("leaf", None, None, None, "grid", None),
        P(),
        P(),
        P(),
        P("leaf", None, None, "grid", None),
    )
    out_specs = (
        P("leaf", None, None, None, "grid", None),
        P("leaf", None, None, None, "grid", None),
    )
    return jax.shard_map(body, mesh=mesh, in_specs=in_specs, out_specs=out_specs, check_vma=False)
```

```python
import functools

import jax
import jax.numpy as jnp
from jax import lax
from jax.experimental import pallas as pl
from jax.experimental.pallas import tpu as pltpu
from jax.sharding import PartitionSpec as P

NB = 128
PB = 8
FB = 16
HALF = PB * NB
QUART = HALF // 2
F = FB * NB
VLIMIT = 56 << 20
f32 = jnp.float32
bf16 = jnp.bfloat16


def iota(shape, axis):
    return lax.broadcasted_iota(jnp.int32, shape, axis)


def split(x):
    high = x.astype(bf16)
    return high, (x - high.astype(f32)).astype(bf16)


def dot_nt(a, b):
    return lax.dot_general(a, b, (((1,), (1,)), ((), ())), preferred_element_type=f32)


def dot3(ah, al, bh, bl):
    return dot_nt(ah, bh) + (dot_nt(ah, bl) + dot_nt(al, bh))


def inverse_factor(block, width):
    groups = [block[8 * i : 8 * i + 8, :] for i in range(16)]
    lane = iota((8, NB), 1)
    sub = iota((8, NB), 0)
    own = width // 8
    for step in range(NB // width):
        first = width * step
        top = first // 8
        inside = (lane >= first) & (lane < first + width)
        spread = {}
        for i in range(top, 16):
            for j in range(width):
                if i < top + own and 8 * (i - top) + 7 < j:
                    continue
                spread[i, j] = jnp.broadcast_to(
                    groups[i][:, first + j : first + j + 1], (8, NB)
                )
        diag = {}
        for a in range(width):
            for b in range(a + 1):
                diag[a, b] = jnp.broadcast_to(
                    spread[top + a // 8, b][a % 8 : a % 8 + 1, :], (8, NB)
                )
        rows = []
        for a in range(width):
            row = jnp.broadcast_to(groups[top + a // 8][a % 8 : a % 8 + 1, :], (8, NB))
            rows.append(jnp.where(lane == first + a, 1.0, jnp.where(inside, 0.0, row)))
        recip = {}
        mult = {}
        for j in range(width):
            recip[j] = 1.0 / diag[j, j]
            for a in range(j + 1, width):
                mult[a, j] = diag[a, j] * recip[j]
            for b in range(j + 1, width):
                for a in range(b, width):
                    diag[a, b] = diag[a, b] - mult[a, j] * diag[b, j]
        solved = []
        for a in range(width):
            row = rows[a]
            for b in range(a):
                row = row - mult[a, b] * solved[b]
            solved.append(row)
        for q in range(own):
            total = None
            for s in range(8):
                a = 8 * q + s
                value = solved[a] * lax.rsqrt(diag[a, a])
                total = value if total is None else jnp.where(sub == s, value, total)
            groups[top + q] = total
        back = [None] * width
        for a in reversed(range(width)):
            row = solved[a] * recip[a]
            for b in reversed(range(a + 1, width)):
                row = row - mult[b, a] * back[b]
            back[a] = row
        for i in range(top + own, 16):
            row = jnp.where(inside, 0.0, groups[i])
            for b in reversed(range(width)):
                row = row - spread[i, b] * back[b]
            groups[i] = row
    return groups


def dot3_cat(ah, al, both):
    wide = dot_nt(ah, both)
    return wide[:, :NB] + (wide[:, NB:] + dot_nt(al, both[:NB, :]))


def factor_half(m, lh, ll, xcat, start, origin, blocks, active):
    lower = iota((NB, NB), 0) >= iota((NB, NB), 1)
    eye = iota((NB, NB), 0) == iota((NB, NB), 1)
    base = start * NB

    def solve(k, r, count):
        lo = k * NB
        rows = slice(r * NB, (r + count) * NB)
        ch, cl = split(m[rows, lo : lo + NB])
        part = dot3_cat(ch, cl, xcat[origin + k - start])
        if r == k:
            part = jnp.where(lower, part, 0.0)
        m[rows, lo : lo + NB] = part
        ph, plow = split(part)
        lh[rows, lo : lo + NB] = ph
        ll[rows, lo : lo + NB] = plow

    def update(k, r, count):
        nxt = k * NB + NB
        cols = slice(base, nxt)
        rows = slice(r * NB, (r + count) * NB)
        both = jnp.concatenate([lh[nxt : nxt + NB, cols], ll[nxt : nxt + NB, cols]], axis=0)
        change = dot3_cat(lh[rows, cols], ll[rows, cols], both)
        m[rows, nxt : nxt + NB] = m[rows, nxt : nxt + NB] - change

    def bulk(k):
        for r in range(k + 2, blocks, 2):
            solve(k, r, min(2, blocks - r))
        if k + 1 < start + 4:
            for r in range(k + 2, blocks, 2):
                update(k, r, min(2, blocks - r))

    def store(k, i, value):
        high, low = split(value)
        count = value.shape[0]
        xcat[origin + k - start, 8 * i : 8 * i + count, :] = high
        xcat[origin + k - start, NB + 8 * i : NB + 8 * i + count, :] = low

    def invert(k, work):
        where = slice(k * NB, k * NB + NB)
        busy = active(k)

        @pl.when(busy)
        def _():
            groups = inverse_factor(m[where, where], 8)
            lane = iota((8, NB), 1)
            for i in range(0, 16, 2):
                pair = [
                    jnp.where(lane <= iota((8, NB), 0) + 8 * j, groups[j], 0.0) for j in (i, i + 1)
                ]
                store(k, i, jnp.concatenate(pair, axis=0))
            work()

        @pl.when(jnp.logical_not(busy))
        def _():
            store(k, 0, jnp.where(eye, lax.rsqrt(m[where, where]), 0.0))
            work()

    invert(start, lambda: None)
    for k in range(start, start + 4):
        solve(k, k, 1)
        if k + 1 < blocks:
            solve(k, k + 1, 1)
        if k + 1 < start + 4:
            update(k, k + 1, 1)
            invert(k + 1, functools.partial(bulk, k))
        else:
            bulk(k)


def subtract_square(m, lh, ll, row0, rows, col0, cols, left):
    wide = 2 * NB
    for c in range(col0, col0 + cols, wide):
        for r in range(max(row0, c), row0 + rows, wide):
            change = dot3(
                lh[r : r + wide, left], ll[r : r + wide, left], lh[c : c + wide, left], ll[c : c + wide, left]
            )
            m[r : r + wide, c : c + wide] = m[r : r + wide, c : c + wide] - change


def prepare_kernel(meta, front, shift, first_out, second_out):
    g = meta[0]
    eye = (iota((NB, NB), 0) == iota((NB, NB), 1)).astype(f32)

    def alive(block):
        return meta[2 + block].astype(f32)

    def sym(out, base, col, start):
        here = alive(start + g)
        for s in range(5):
            r = (g + s) % PB
            off = pl.multiple_of((start + r) * NB, NB)
            block = front[pl.ds(off, NB), col * NB : col * NB + NB]
            block = block * (here * alive(start + r))
            if s == 0:
                block = block + eye * (1.0 - here)

            @pl.when(r >= g)
            def _():
                out[base + s * NB : base + s * NB + NB, :] = block

            @pl.when(r < g)
            def _():
                out[base + s * NB : base + s * NB + NB, :] = block.T

    sym(first_out, 0, 0, 0)
    first_out[5 * NB : 5 * NB + 8, :] = jnp.broadcast_to(shift[0:1, :], (8, NB))
    here = alive(g)
    for r in range(PB):
        rows = slice(HALF + r * NB, HALF + r * NB + NB)
        second_out[r * NB : r * NB + NB, :] = front[rows, :NB] * (here * alive(PB + r))
    sym(second_out, HALF, 1, PB)


OFFSETS = ((0, 0), (0, 3), (0, 1), (0, 2), (1, 0), (1, 3), (1, 1), (1, 2))


def holder_of(meta, k):
    g = meta[0]
    dx, dz = OFFSETS[k]
    return (g // 4 ^ dx) * 4 + (g % 4 + dz) % 4


def place_sym(meta, parts, base, target):
    for k in range(PB):
        h = holder_of(meta, k)
        for s in range(5):
            r = (h + s) % PB
            row = pl.multiple_of(jnp.maximum(r, h) * NB, NB)
            col = pl.multiple_of(jnp.minimum(r, h) * NB, NB)
            target[pl.ds(row, NB), pl.ds(col, NB)] = parts[k][
                base + s * NB : base + s * NB + NB, :
            ]


def child_first_kernel(meta, *refs):
    parts = refs[:PB]
    lh, ll, xcat, column, shifts, rest, m = refs[PB:]
    g = meta[0]
    place_sym(meta, parts, 0, m)
    shifts[...] = jnp.zeros_like(shifts)
    for k in range(PB):
        off = pl.multiple_of(holder_of(meta, k) * NB, NB)
        shifts[:, pl.ds(off, NB)] = parts[k][5 * NB : 5 * NB + 8, :]
    rest[...] = m[QUART:, QUART:]
    lh[...] = jnp.zeros_like(lh)
    ll[...] = jnp.zeros_like(ll)
    factor_half(m, lh, ll, xcat, 0, 0, PB, lambda k: meta[2 + k] > 0)

    @pl.when(g < 4)
    def _():
        mine = pl.multiple_of(g * NB, NB)
        for r in range(PB):
            block = m[r * NB : r * NB + NB, pl.ds(mine, NB)]
            column[r * NB : r * NB + NB, :] = jnp.where(r >= g, block, 0.0)


def child_second_kernel(meta, rest, ah, al, lh, ll, xcat, column, m):
    g = meta[0]
    m[...] = rest[...]
    wide = 2 * NB
    for c in range(0, QUART, wide):
        for r in range(c, QUART, wide):
            change = dot3(
                ah[QUART + r : QUART + r + wide, :],
                al[QUART + r : QUART + r + wide, :],
                ah[QUART + c : QUART + c + wide, :],
                al[QUART + c : QUART + c + wide, :],
            )
            m[r : r + wide, c : c + wide] = m[r : r + wide, c : c + wide] - change
    lh[...] = jnp.zeros_like(lh)
    ll[...] = jnp.zeros_like(ll)
    factor_half(m, lh, ll, xcat, 0, 0, 4, lambda k: meta[6 + k] > 0)

    @pl.when(g >= 4)
    def _():
        mine = pl.multiple_of((g - 4) * NB, NB)
        for r in range(4):
            block = m[r * NB : r * NB + NB, pl.ds(mine, NB)]
            column[r * NB : r * NB + NB, :] = jnp.where(r >= g - 4, block, 0.0)


def solve_quarter(m, bh, bl, lh, ll, xcat, base):
    step = 2 * NB

    def block(k):
        lo = base + k * NB
        for r in range(0, HALF, step):
            ch, cl = split(m[r : r + step, lo : lo + NB])
            part = dot3_cat(ch, cl, xcat[k])
            m[r : r + step, lo : lo + NB] = part
            ph, plow = split(part)
            bh[r : r + step, lo : lo + NB] = ph
            bl[r : r + step, lo : lo + NB] = plow

    def update(first, count):
        left = slice(base + first * NB, base + (first + count) * NB)
        inner = slice(first * NB, (first + count) * NB)
        target = slice((first + count) * NB, (first + 2 * count) * NB)
        out = slice(base + target.start, base + target.stop)
        th = lh[target, inner]
        tl = ll[target, inner]
        for r in range(0, HALF, step):
            rows = slice(r, r + step)
            m[rows, out] = m[rows, out] - dot3(bh[rows, left], bl[rows, left], th, tl)

    block(0)
    update(0, 1)
    block(1)
    update(0, 2)
    block(2)
    update(2, 1)
    block(3)


def child_third_kernel(meta, ah, al, xa, ca, shifts, lh, ll, xb, cb, *refs):
    parts = refs[:PB]
    factor, schur, m, bh, bl = refs[PB:]
    g = meta[0]
    for k in range(PB):
        off = pl.multiple_of(holder_of(meta, k) * NB, NB)
        m[:, pl.ds(off, NB)] = parts[k][:HALF, :]
    place_sym(meta, parts, HALF, schur)
    schur[HALF : HALF + 8, :] = shifts[...]
    solve_quarter(m, bh, bl, ah, al, xa, 0)
    th = ah[QUART:, :]
    tl = al[QUART:, :]
    for r in range(0, HALF, 2 * NB):
        rows = slice(r, r + 2 * NB)
        m[rows, QUART:] = m[rows, QUART:] - dot3(bh[rows, :QUART], bl[rows, :QUART], th, tl)
    solve_quarter(m, bh, bl, lh, ll, xb, QUART)
    subtract_square(schur, bh, bl, 0, HALF, 0, HALF, slice(0, HALF))

    @pl.when(g < 4)
    def _():
        factor[:HALF, :] = ca[...]

    @pl.when(g >= 4)
    def _():
        factor[:QUART, :] = jnp.zeros((QUART, NB), f32)
        factor[QUART:HALF, :] = cb[...]

    factor[HALF:, :] = m[:, pl.ds(pl.multiple_of(g * NB, NB), NB)]


def parent_kernel(meta, own, other, out, m, lh, ll, xcat, inverse):
    g = meta[0]
    member = meta[1]
    slot = member * PB + g
    for side in range(2):
        for q in range(FB):
            inverse[side, q] = -1
        for c in range(PB):
            live = meta[2 + 16 * side + PB + c]
            dest = meta[34 + 8 * side + c]
            inverse[side, dest] = jnp.where(live > 0, c, -1)
    mine = jnp.int32(0)
    for q in range(FB):
        mine = jnp.where(meta[50 + q] == slot, q, mine)
    sides = (own, other)
    eye = iota((NB, NB), 0) == iota((NB, NB), 1)

    def diagonal(block):
        holder = meta[50 + block]
        off = pl.multiple_of(holder % PB * NB, NB)
        a = own[HALF : HALF + 1, pl.ds(off, NB)]
        b = other[HALF : HALF + 1, pl.ds(off, NB)]
        row = jnp.where(holder // PB == member, a, b)
        return jnp.where(eye, jnp.broadcast_to(row, (NB, NB)), 0.0)

    for p in range(PB):
        for q in range(p, FB):
            where = (slice(q * NB, q * NB + NB), slice(p * NB, p * NB + NB))
            m[where] = diagonal(p) if p == q else jnp.zeros((NB, NB), f32)
            for side in range(2):
                ci = inverse[side, q]
                cj = inverse[side, p]

                @pl.when((ci >= 0) & (cj >= 0))
                def _():
                    ro = pl.multiple_of(ci * NB, NB)
                    co = pl.multiple_of(cj * NB, NB)
                    m[where] = m[where] + sides[side][pl.ds(ro, NB), pl.ds(co, NB)]

    lh[...] = jnp.zeros_like(lh)
    ll[...] = jnp.zeros_like(ll)


    def touched(p):
        return (inverse[0, p] >= 0) | (inverse[1, p] >= 0)

    factor_half(m, lh, ll, xcat, 0, 0, FB, touched)
    subtract_square(m, lh, ll, QUART, F - QUART, QUART, QUART, slice(0, QUART))
    factor_half(m, lh, ll, xcat, 4, 4, FB, touched)

    @pl.when(mine < PB)
    def _():
        off = pl.multiple_of(mine * NB, NB)
        for r in range(FB):
            block = m[r * NB : r * NB + NB, pl.ds(off, NB)]
            out[r * NB : r * NB + NB, :] = jnp.where(r >= mine, block, 0.0)

    @pl.when(mine >= PB)
    def _():
        out[:HALF, :] = jnp.zeros((HALF, NB), f32)
        off = pl.multiple_of(mine * NB, NB)
        rh = lh[pl.ds(off, NB), :]
        rl = ll[pl.ds(off, NB), :]
        diag = diagonal(mine)
        for q in range(PB, FB):
            rows = slice(q * NB, q * NB + NB)
            out[rows, :] = jnp.where(mine == q, diag, 0.0) - dot3(
                lh[rows, :], ll[rows, :], rh, rl
            )
            for side in range(2):
                ci = inverse[side, q]
                cj = inverse[side, mine]
                high = pl.multiple_of(jnp.maximum(jnp.maximum(ci, cj), 0) * NB, NB)
                low = pl.multiple_of(jnp.maximum(jnp.minimum(ci, cj), 0) * NB, NB)

                @pl.when((ci >= cj) & (cj >= 0))
                def _():
                    out[rows, :] = out[rows, :] + sides[side][pl.ds(high, NB), pl.ds(low, NB)]

                @pl.when((ci >= 0) & (ci < cj))
                def _():
                    out[rows, :] = out[rows, :] + sides[side][pl.ds(high, NB), pl.ds(low, NB)].T


VM = pl.BlockSpec(memory_space=pltpu.VMEM)
SM = pl.BlockSpec(memory_space=pltpu.SMEM)


def shape(*dims, dtype=f32):
    return jax.ShapeDtypeStruct(dims, dtype)


def run(kernel, outs, scratch, flops, meta, *args):
    return pl.pallas_call(
        kernel,
        out_shape=outs,
        in_specs=[SM] + [VM] * len(args),
        out_specs=jax.tree.map(lambda _: VM, outs),
        scratch_shapes=scratch,
        compiler_params=pltpu.CompilerParams(vmem_limit_bytes=VLIMIT),
        cost_estimate=pl.CostEstimate(flops=flops, bytes_accessed=1 << 22, transcendentals=0),
    )(meta, *args)


def permute(value, dx, dz):
    pairs = [(x * 4 + z, (x ^ dx) * 4 + (z + dz) % 4) for x in range(2) for z in range(4)]
    return lax.ppermute(value, "grid", pairs)


def near(value):
    return [value] + [permute(value, 0, 1), permute(value, 0, 3), permute(value, 0, 2), permute(value, 1, 0)]


def far(parts):
    third, side = parts[3], parts[4]
    return parts + [permute(side, 0, 1), permute(side, 0, 3), permute(third, 1, 0)]


def body(child_front, child_live, child_map, parent_owner, parent_shift):
    g = lax.axis_index("grid").astype(jnp.int32)
    leaf = lax.axis_index("leaf").astype(jnp.int32)
    sibling = leaf ^ 1

    def row(table, index):
        return lax.dynamic_index_in_dim(table.reshape(table.shape[0], -1), index, 0, keepdims=False)

    meta = jnp.concatenate(
        [
            jnp.stack([g, leaf % 2]),
            row(child_live, leaf),
            row(child_live, sibling),
            row(child_map, leaf),
            row(child_map, sibling),
            row(parent_owner, leaf // 2),
        ]
    )
    front = child_front.reshape(F, 2 * NB)
    shift = parent_shift.reshape(1, NB)
    first, second = run(
        prepare_kernel,
        (shape(5 * NB + 8, NB), shape(HALF + 5 * NB, NB)),
        [],
        1 << 20,
        meta,
        front,
        shift,
    )
    first_parts = far(near(first))
    first_parts, second = lax.optimization_barrier((first_parts, second))
    second_near = near(second)
    ah, al, xa, ca, shifts, rest = run(
        child_first_kernel,
        (
            shape(HALF, QUART, dtype=bf16),
            shape(HALF, QUART, dtype=bf16),
            shape(4, 2 * NB, NB, dtype=bf16),
            shape(HALF, NB),
            shape(8, HALF),
            shape(QUART, QUART),
        ),
        [pltpu.VMEM((HALF, HALF), f32)],
        20 * 10**9,
        meta,
        *first_parts,
    )
    second_near, rest = lax.optimization_barrier((second_near, rest))
    second_parts = far(second_near)
    lh, ll, xb, cb = run(
        child_second_kernel,
        (
            shape(QUART, QUART, dtype=bf16),
            shape(QUART, QUART, dtype=bf16),
            shape(4, 2 * NB, NB, dtype=bf16),
            shape(QUART, NB),
        ),
        [pltpu.VMEM((QUART, QUART), f32)],
        20 * 10**9,
        meta,
        rest,
        ah,
        al,
    )
    factor, schur = run(
        child_third_kernel,
        (shape(F, NB), shape(HALF + 8, HALF)),
        [
            pltpu.VMEM((HALF, HALF), f32),
            pltpu.VMEM((HALF, HALF), bf16),
            pltpu.VMEM((HALF, HALF), bf16),
        ],
        10**10,
        meta,
        ah,
        al,
        xa,
        ca,
        shifts,
        lh,
        ll,
        xb,
        cb,
        *second_parts,
    )
    other = lax.ppermute(schur, "leaf", [(s, s ^ 1) for s in range(lax.axis_size("leaf"))])
    done = run(
        parent_kernel,
        shape(F, NB),
        [
            pltpu.VMEM((F, HALF), f32),
            pltpu.VMEM((F, HALF), bf16),
            pltpu.VMEM((F, HALF), bf16),
            pltpu.VMEM((PB, 2 * NB, NB), bf16),
            pltpu.SMEM((2, FB), jnp.int32),
        ],
        40 * 10**9,
        meta,
        schur,
        other,
    )
    return factor.reshape(1, 1, F, 1, 1, NB), done.reshape(1, 1, F, 1, 1, NB)


def solution(mesh):
    in_specs = (
        P("leaf", None, None, None, "grid", None),
        P(),
        P(),
        P(),
        P("leaf", None, None, "grid", None),
    )
    out_specs = (
        P("leaf", None, None, None, "grid", None),
        P("leaf", None, None, None, "grid", None),
    )
    return jax.shard_map(body, mesh=mesh, in_specs=in_specs, out_specs=out_specs, check_vma=False)
```

```python
import functools

import jax
import jax.numpy as jnp
from jax import lax
from jax.experimental import pallas as pl
from jax.experimental.pallas import tpu as pltpu
from jax.sharding import PartitionSpec as P

NB = 128
PB = 8
FB = 16
HALF = PB * NB
QUART = HALF // 2
F = FB * NB
VLIMIT = 56 << 20
f32 = jnp.float32
bf16 = jnp.bfloat16


HALF_BLOCK = NB // 2
SYM = 4 * NB + HALF_BLOCK
PACKED = PB * (PB + 1) // 2 * NB


class Meta:
    def __init__(self, place, live, dest, owner):
        self.g = place[0]
        self.leaf = place[1]
        self.member = place[1] % 2
        self.live_table = live
        self.dest_table = dest
        self.owner_table = owner

    def live(self, block, side=0):
        return self.live_table[self.leaf ^ side, 0, block]

    def dest(self, block, side):
        return self.dest_table[self.leaf ^ side, 0, block]

    def owner(self, block):
        return self.owner_table[self.leaf // 2, block]


def packed(row, col):
    return pl.multiple_of((row * (row + 1) // 2 + col) * NB, NB)


def iota(shape, axis):
    return lax.broadcasted_iota(jnp.int32, shape, axis)


def split(x):
    high = x.astype(bf16)
    return high, (x - high.astype(f32)).astype(bf16)


def dot_nt(a, b):
    return lax.dot_general(a, b, (((1,), (1,)), ((), ())), preferred_element_type=f32)


def dot3(ah, al, bh, bl):
    return dot_nt(ah, bh) + (dot_nt(ah, bl) + dot_nt(al, bh))


def inverse_factor(block, width):
    groups = [block[8 * i : 8 * i + 8, :] for i in range(16)]
    lane = iota((8, NB), 1)
    sub = iota((8, NB), 0)
    own = width // 8
    for step in range(NB // width):
        first = width * step
        top = first // 8
        inside = (lane >= first) & (lane < first + width)
        spread = {}
        for i in range(top, 16):
            for j in range(width):
                if i < top + own and 8 * (i - top) + 7 < j:
                    continue
                spread[i, j] = jnp.broadcast_to(
                    groups[i][:, first + j : first + j + 1], (8, NB)
                )
        diag = {}
        for a in range(width):
            for b in range(a + 1):
                diag[a, b] = jnp.broadcast_to(
                    spread[top + a // 8, b][a % 8 : a % 8 + 1, :], (8, NB)
                )
        rows = []
        for a in range(width):
            row = jnp.broadcast_to(groups[top + a // 8][a % 8 : a % 8 + 1, :], (8, NB))
            rows.append(jnp.where(lane == first + a, 1.0, jnp.where(inside, 0.0, row)))
        recip = {}
        mult = {}
        for j in range(width):
            recip[j] = 1.0 / diag[j, j]
            for a in range(j + 1, width):
                mult[a, j] = diag[a, j] * recip[j]
            for b in range(j + 1, width):
                for a in range(b, width):
                    diag[a, b] = diag[a, b] - mult[a, j] * diag[b, j]
        solved = []
        for a in range(width):
            row = rows[a]
            for b in range(a):
                row = row - mult[a, b] * solved[b]
            solved.append(row)
        for q in range(own):
            total = None
            for s in range(8):
                a = 8 * q + s
                value = solved[a] * lax.rsqrt(diag[a, a])
                total = value if total is None else jnp.where(sub == s, value, total)
            groups[top + q] = total
        back = [None] * width
        for a in reversed(range(width)):
            row = solved[a] * recip[a]
            for b in reversed(range(a + 1, width)):
                row = row - mult[b, a] * back[b]
            back[a] = row
        for i in range(top + own, 16):
            row = jnp.where(inside, 0.0, groups[i])
            for b in reversed(range(width)):
                row = row - spread[i, b] * back[b]
            groups[i] = row
    return groups


def dot3_cat(ah, al, both):
    wide = dot_nt(ah, both)
    return wide[:, :NB] + (wide[:, NB:] + dot_nt(al, both[:NB, :]))


def factor_half(m, lh, ll, xcat, start, origin, blocks, active):
    lower = iota((NB, NB), 0) >= iota((NB, NB), 1)
    eye = iota((NB, NB), 0) == iota((NB, NB), 1)
    base = start * NB

    def solve(k, r, count):
        lo = k * NB
        rows = slice(r * NB, (r + count) * NB)
        ch, cl = split(m[rows, lo : lo + NB])
        part = dot3_cat(ch, cl, xcat[origin + k - start])
        if r == k:
            part = jnp.where(lower, part, 0.0)
        m[rows, lo : lo + NB] = part
        ph, plow = split(part)
        lh[rows, lo : lo + NB] = ph
        ll[rows, lo : lo + NB] = plow

    def update(k, r, count):
        nxt = k * NB + NB
        cols = slice(base, nxt)
        rows = slice(r * NB, (r + count) * NB)
        both = jnp.concatenate([lh[nxt : nxt + NB, cols], ll[nxt : nxt + NB, cols]], axis=0)
        change = dot3_cat(lh[rows, cols], ll[rows, cols], both)
        m[rows, nxt : nxt + NB] = m[rows, nxt : nxt + NB] - change

    def bulk(k):
        for r in range(k + 2, blocks, 2):
            solve(k, r, min(2, blocks - r))
        if k + 1 < start + 4:
            for r in range(k + 2, blocks, 2):
                update(k, r, min(2, blocks - r))

    def store(k, i, value):
        high, low = split(value)
        count = value.shape[0]
        xcat[origin + k - start, 8 * i : 8 * i + count, :] = high
        xcat[origin + k - start, NB + 8 * i : NB + 8 * i + count, :] = low

    def invert(k, work):
        where = slice(k * NB, k * NB + NB)
        busy = active(k)

        @pl.when(busy)
        def _():
            groups = inverse_factor(m[where, where], 8)
            lane = iota((8, NB), 1)
            for i in range(0, 16, 2):
                pair = [
                    jnp.where(lane <= iota((8, NB), 0) + 8 * j, groups[j], 0.0) for j in (i, i + 1)
                ]
                store(k, i, jnp.concatenate(pair, axis=0))
            work()

        @pl.when(jnp.logical_not(busy))
        def _():
            store(k, 0, jnp.where(eye, lax.rsqrt(m[where, where]), 0.0))
            work()

    invert(start, lambda: None)
    for k in range(start, start + 4):
        solve(k, k, 1)
        if k + 1 < blocks:
            solve(k, k + 1, 1)
        if k + 1 < start + 4:
            update(k, k + 1, 1)
            invert(k + 1, functools.partial(bulk, k))
        else:
            bulk(k)


def subtract_square(m, lh, ll, row0, rows, col0, cols, left):
    wide = 2 * NB
    for c in range(col0, col0 + cols, wide):
        for r in range(max(row0, c), row0 + rows, wide):
            change = dot3(
                lh[r : r + wide, left], ll[r : r + wide, left], lh[c : c + wide, left], ll[c : c + wide, left]
            )
            m[r : r + wide, c : c + wide] = m[r : r + wide, c : c + wide] - change


def prepare_kernel(meta, front, shift, first_out, second_out):
    g = meta.g
    eye = (iota((NB, NB), 0) == iota((NB, NB), 1)).astype(f32)

    def alive(block):
        return meta.live(block).astype(f32)

    def column(first, col):
        return front[pl.ds(pl.multiple_of(first * 2, 8) + col, NB, stride=2), :]

    def sym(out, base, col, start):
        here = alive(start + g)
        for s in range(5):
            r = (g + s) % PB
            block = column((start + r) * NB, col)
            block = block * (here * alive(start + r))
            if s == 0:
                block = block + eye * (1.0 - here)

            @pl.when(r >= g)
            def _():
                count = NB if s < 4 else HALF_BLOCK
                out[base + s * NB : base + s * NB + count, :] = block[:count, :]

            @pl.when(r < g)
            def _():
                skip = 0 if s < 4 else HALF_BLOCK
                out[base + s * NB : base + (s + 1) * NB - skip, :] = block.T[skip:, :]

    sym(first_out, 0, 0, 0)
    first_out[SYM : SYM + 8, :] = jnp.broadcast_to(shift[0:1, :], (8, NB))
    here = alive(g)
    for r in range(PB):
        second_out[r * NB : r * NB + NB, :] = column(HALF + r * NB, 0) * (here * alive(PB + r))
    sym(second_out, HALF, 1, PB)


OFFSETS = ((0, 0), (0, 3), (0, 1), (0, 2), (1, 0), (1, 3), (1, 1), (1, 2))


def holder_of(meta, k):
    g = meta.g
    dx, dz = OFFSETS[k]
    return (g // 4 ^ dx) * 4 + (g % 4 + dz) % 4


def place_sym(meta, parts, base, target, address):
    for k in range(PB):
        h = holder_of(meta, k)
        for s in range(5):
            r = (h + s) % PB
            row, cols = address(jnp.maximum(r, h), jnp.minimum(r, h))
            count = NB
            if s == 4:
                count = HALF_BLOCK
                row = pl.multiple_of(row + jnp.where(r >= h, 0, HALF_BLOCK), HALF_BLOCK)
            target[pl.ds(row, count), cols] = parts[k][base + s * NB : base + s * NB + count, :]


def child_first_kernel(meta, *refs):
    parts = refs[:PB]
    lh, ll, xcat, column, shifts, rest, m = refs[PB:]
    g = meta.g
    place_sym(
        meta,
        parts,
        0,
        m,
        lambda r, c: (pl.multiple_of(r * NB, NB), pl.ds(pl.multiple_of(c * NB, NB), NB)),
    )
    for k in range(PB):
        shifts[pl.ds(holder_of(meta, k), 1), :] = parts[k][SYM : SYM + 1, :]
    rest[...] = m[QUART:, QUART:]
    lh[...] = jnp.zeros_like(lh)
    ll[...] = jnp.zeros_like(ll)
    factor_half(m, lh, ll, xcat, 0, 0, PB, lambda k: meta.live(k) > 0)

    @pl.when(g < 4)
    def _():
        mine = pl.multiple_of(g * NB, NB)
        for r in range(PB):
            block = m[r * NB : r * NB + NB, pl.ds(mine, NB)]
            column[r * NB : r * NB + NB, :] = jnp.where(r >= g, block, 0.0)


def child_second_kernel(meta, rest, ah, al, lh, ll, xcat, column, m):
    g = meta.g
    m[...] = rest[...]
    wide = 2 * NB
    for c in range(0, QUART, wide):
        for r in range(c, QUART, wide):
            change = dot3(
                ah[QUART + r : QUART + r + wide, :],
                al[QUART + r : QUART + r + wide, :],
                ah[QUART + c : QUART + c + wide, :],
                al[QUART + c : QUART + c + wide, :],
            )
            m[r : r + wide, c : c + wide] = m[r : r + wide, c : c + wide] - change
    lh[...] = jnp.zeros_like(lh)
    ll[...] = jnp.zeros_like(ll)
    factor_half(m, lh, ll, xcat, 0, 0, 4, lambda k: meta.live(4 + k) > 0)

    @pl.when(g >= 4)
    def _():
        mine = pl.multiple_of((g - 4) * NB, NB)
        for r in range(4):
            block = m[r * NB : r * NB + NB, pl.ds(mine, NB)]
            column[r * NB : r * NB + NB, :] = jnp.where(r >= g - 4, block, 0.0)


def solve_quarter(m, bh, bl, lh, ll, xcat, base):
    step = 2 * NB

    def block(k):
        lo = base + k * NB
        for r in range(0, HALF, step):
            ch, cl = split(m[r : r + step, lo : lo + NB])
            part = dot3_cat(ch, cl, xcat[k])
            m[r : r + step, lo : lo + NB] = part
            ph, plow = split(part)
            bh[r : r + step, lo : lo + NB] = ph
            bl[r : r + step, lo : lo + NB] = plow

    def update(first, count):
        left = slice(base + first * NB, base + (first + count) * NB)
        inner = slice(first * NB, (first + count) * NB)
        target = slice((first + count) * NB, (first + 2 * count) * NB)
        out = slice(base + target.start, base + target.stop)
        th = lh[target, inner]
        tl = ll[target, inner]
        for r in range(0, HALF, step):
            rows = slice(r, r + step)
            m[rows, out] = m[rows, out] - dot3(bh[rows, left], bl[rows, left], th, tl)

    block(0)
    update(0, 1)
    block(1)
    update(0, 2)
    block(2)
    update(2, 1)
    block(3)


def child_third_kernel(meta, ah, al, xa, ca, shifts, lh, ll, xb, cb, *refs):
    parts = refs[:PB]
    factor, schur, m, bh, bl = refs[PB:]
    g = meta.g
    for k in range(PB):
        off = pl.multiple_of(holder_of(meta, k) * NB, NB)
        m[:, pl.ds(off, NB)] = parts[k][:HALF, :]
    place_sym(meta, parts, HALF, schur, lambda r, c: (packed(r, c), slice(None)))
    schur[PACKED : PACKED + 8, :] = shifts[...]
    solve_quarter(m, bh, bl, ah, al, xa, 0)
    th = ah[QUART:, :]
    tl = al[QUART:, :]
    for r in range(0, HALF, 2 * NB):
        rows = slice(r, r + 2 * NB)
        m[rows, QUART:] = m[rows, QUART:] - dot3(bh[rows, :QUART], bl[rows, :QUART], th, tl)
    solve_quarter(m, bh, bl, lh, ll, xb, QUART)
    for c in range(0, PB, 2):
        cols = slice(c * NB, (c + 2) * NB)
        for r in range(c, PB, 2):
            rows = slice(r * NB, (r + 2) * NB)
            change = dot3(bh[rows, :], bl[rows, :], bh[cols, :], bl[cols, :])
            for i in range(2):
                for j in range(2):
                    if r + i >= c + j:
                        at = ((r + i) * (r + i + 1) // 2 + c + j) * NB
                        part = change[i * NB : i * NB + NB, j * NB : j * NB + NB]
                        schur[at : at + NB, :] = schur[at : at + NB, :] - part

    @pl.when(g < 4)
    def _():
        factor[:HALF, :] = ca[...]

    @pl.when(g >= 4)
    def _():
        factor[:QUART, :] = jnp.zeros((QUART, NB), f32)
        factor[QUART:HALF, :] = cb[...]

    factor[HALF:, :] = m[:, pl.ds(pl.multiple_of(g * NB, NB), NB)]


def parent_kernel(meta, own, other, out, m, lh, ll, xcat, inverse):
    g = meta.g
    member = meta.member
    slot = member * PB + g
    for side in range(2):
        for q in range(FB):
            inverse[side, q] = -1
        for c in range(PB):
            live = meta.live(PB + c, side)
            dest = meta.dest(c, side)
            inverse[side, dest] = jnp.where(live > 0, c, -1)
    mine = jnp.int32(0)
    for q in range(FB):
        mine = jnp.where(meta.owner(q) == slot, q, mine)
    sides = (own, other)
    eye = iota((NB, NB), 0) == iota((NB, NB), 1)

    def diagonal(block):
        holder = meta.owner(block)
        a = own[pl.ds(PACKED + holder % PB, 1), :]
        b = other[pl.ds(PACKED + holder % PB, 1), :]
        row = jnp.where(holder // PB == member, a, b)
        return jnp.where(eye, jnp.broadcast_to(row, (NB, NB)), 0.0)

    for p in range(PB):
        for q in range(p, FB):
            where = (slice(q * NB, q * NB + NB), slice(p * NB, p * NB + NB))
            m[where] = diagonal(p) if p == q else jnp.zeros((NB, NB), f32)
            for side in range(2):
                ci = inverse[side, q]
                cj = inverse[side, p]

                @pl.when((ci >= 0) & (cj >= 0))
                def _():
                    m[where] = m[where] + sides[side][pl.ds(packed(ci, cj), NB), :]

    lh[...] = jnp.zeros_like(lh)
    ll[...] = jnp.zeros_like(ll)


    def touched(p):
        return (inverse[0, p] >= 0) | (inverse[1, p] >= 0)

    factor_half(m, lh, ll, xcat, 0, 0, FB, touched)
    subtract_square(m, lh, ll, QUART, F - QUART, QUART, QUART, slice(0, QUART))
    factor_half(m, lh, ll, xcat, 4, 4, FB, touched)

    @pl.when(mine < PB)
    def _():
        off = pl.multiple_of(mine * NB, NB)
        for r in range(FB):
            block = m[r * NB : r * NB + NB, pl.ds(off, NB)]
            out[r * NB : r * NB + NB, :] = jnp.where(r >= mine, block, 0.0)

    @pl.when(mine >= PB)
    def _():
        out[:HALF, :] = jnp.zeros((HALF, NB), f32)
        off = pl.multiple_of(mine * NB, NB)
        rh = lh[pl.ds(off, NB), :]
        rl = ll[pl.ds(off, NB), :]
        diag = diagonal(mine)
        for q in range(PB, FB):
            rows = slice(q * NB, q * NB + NB)
            out[rows, :] = jnp.where(mine == q, diag, 0.0) - dot3(
                lh[rows, :], ll[rows, :], rh, rl
            )
            for side in range(2):
                ci = inverse[side, q]
                cj = inverse[side, mine]
                high = jnp.maximum(jnp.maximum(ci, cj), 0)
                at = packed(high, jnp.maximum(jnp.minimum(ci, cj), 0))

                @pl.when((ci >= cj) & (cj >= 0))
                def _():
                    out[rows, :] = out[rows, :] + sides[side][pl.ds(at, NB), :]

                @pl.when((ci >= 0) & (ci < cj))
                def _():
                    out[rows, :] = out[rows, :] + sides[side][pl.ds(at, NB), :].T


VM = pl.BlockSpec(memory_space=pltpu.VMEM)
SM = pl.BlockSpec(memory_space=pltpu.SMEM)


def shape(*dims, dtype=f32):
    return jax.ShapeDtypeStruct(dims, dtype)


def run(kernel, outs, scratch, flops, meta, *args):
    def wrapped(place, live, dest, owner, *refs):
        kernel(Meta(place, live, dest, owner), *refs)

    return pl.pallas_call(
        wrapped,
        out_shape=outs,
        in_specs=[SM] * 4 + [VM] * len(args),
        out_specs=jax.tree.map(lambda _: VM, outs),
        scratch_shapes=scratch,
        compiler_params=pltpu.CompilerParams(vmem_limit_bytes=VLIMIT),
        cost_estimate=pl.CostEstimate(flops=flops, bytes_accessed=1 << 22, transcendentals=0),
    )(*meta, *args)


def permute(value, dx, dz):
    pairs = [(x * 4 + z, (x ^ dx) * 4 + (z + dz) % 4) for x in range(2) for z in range(4)]
    return lax.ppermute(value, "grid", pairs)


def near(value):
    return [value] + [permute(value, 0, 1), permute(value, 0, 3), permute(value, 0, 2), permute(value, 1, 0)]


def far(parts):
    third, side = parts[3], parts[4]
    return parts + [permute(side, 0, 1), permute(side, 0, 3), permute(third, 1, 0)]


def body(child_front, child_live, child_map, parent_owner, parent_shift):
    g = lax.axis_index("grid").astype(jnp.int32)
    leaf = lax.axis_index("leaf").astype(jnp.int32)
    meta = (jnp.stack([g, leaf]), child_live, child_map, parent_owner)
    front = child_front.reshape(2 * F, NB)
    shift = parent_shift.reshape(1, NB)
    first, second = run(
        prepare_kernel,
        (shape(SYM + 8, NB), shape(HALF + SYM, NB)),
        [],
        1 << 20,
        meta,
        front,
        shift,
    )
    first_parts = far(near(first))
    first_parts, second = lax.optimization_barrier((first_parts, second))
    second_near = near(second)
    ah, al, xa, ca, shifts, rest = run(
        child_first_kernel,
        (
            shape(HALF, QUART, dtype=bf16),
            shape(HALF, QUART, dtype=bf16),
            shape(4, 2 * NB, NB, dtype=bf16),
            shape(HALF, NB),
            shape(8, NB),
            shape(QUART, QUART),
        ),
        [pltpu.VMEM((HALF, HALF), f32)],
        20 * 10**9,
        meta,
        *first_parts,
    )
    second_near, rest = lax.optimization_barrier((second_near, rest))
    second_parts = far(second_near)
    lh, ll, xb, cb = run(
        child_second_kernel,
        (
            shape(QUART, QUART, dtype=bf16),
            shape(QUART, QUART, dtype=bf16),
            shape(4, 2 * NB, NB, dtype=bf16),
            shape(QUART, NB),
        ),
        [pltpu.VMEM((QUART, QUART), f32)],
        20 * 10**9,
        meta,
        rest,
        ah,
        al,
    )
    factor, schur = run(
        child_third_kernel,
        (shape(F, NB), shape(PACKED + 8, NB)),
        [
            pltpu.VMEM((HALF, HALF), f32),
            pltpu.VMEM((HALF, HALF), bf16),
            pltpu.VMEM((HALF, HALF), bf16),
        ],
        10**10,
        meta,
        ah,
        al,
        xa,
        ca,
        shifts,
        lh,
        ll,
        xb,
        cb,
        *second_parts,
    )
    other = lax.ppermute(schur, "leaf", [(s, s ^ 1) for s in range(lax.axis_size("leaf"))])
    done = run(
        parent_kernel,
        shape(F, NB),
        [
            pltpu.VMEM((F, HALF), f32),
            pltpu.VMEM((F, HALF), bf16),
            pltpu.VMEM((F, HALF), bf16),
            pltpu.VMEM((PB, 2 * NB, NB), bf16),
            pltpu.SMEM((2, FB), jnp.int32),
        ],
        40 * 10**9,
        meta,
        schur,
        other,
    )
    return factor.reshape(1, 1, F, 1, 1, NB), done.reshape(1, 1, F, 1, 1, NB)


def solution(mesh):
    in_specs = (
        P("leaf", None, None, None, "grid", None),
        P(),
        P(),
        P(),
        P("leaf", None, None, "grid", None),
    )
    out_specs = (
        P("leaf", None, None, None, "grid", None),
        P("leaf", None, None, None, "grid", None),
    )
    return jax.shard_map(body, mesh=mesh, in_specs=in_specs, out_specs=out_specs, check_vma=False)
```

```python
import functools

import jax
import jax.numpy as jnp
from jax import lax
from jax.experimental import pallas as pl
from jax.experimental.pallas import tpu as pltpu
from jax.sharding import PartitionSpec as P

NB = 128
PB = 8
FB = 16
HALF = PB * NB
QUART = HALF // 2
F = FB * NB
f32 = jnp.float32
bf16 = jnp.bfloat16


HALF_BLOCK = NB // 2
SYM = 4 * NB + HALF_BLOCK
PACKED = PB * (PB + 1) // 2 * NB


class Meta:
    def __init__(self, place, live, dest, owner):
        self.g = place[0]
        self.leaf = place[1]
        self.member = place[1] % 2
        self.live_table = live
        self.dest_table = dest
        self.owner_table = owner

    def live(self, block, side=0):
        return self.live_table[self.leaf ^ side, 0, block]

    def dest(self, block, side):
        return self.dest_table[self.leaf ^ side, 0, block]

    def owner(self, block):
        return self.owner_table[self.leaf // 2, block]


def packed(row, col):
    return pl.multiple_of((row * (row + 1) // 2 + col) * NB, NB)


def iota(shape, axis):
    return lax.broadcasted_iota(jnp.int32, shape, axis)


def split(x):
    high = x.astype(bf16)
    return high, (x - high.astype(f32)).astype(bf16)


def dot_nt(a, b):
    return lax.dot_general(a, b, (((1,), (1,)), ((), ())), preferred_element_type=f32)


def dot3(ah, al, bh, bl):
    return dot_nt(ah, bh) + (dot_nt(ah, bl) + dot_nt(al, bh))


def inverse_factor(block, width):
    groups = [block[8 * i : 8 * i + 8, :] for i in range(16)]
    lane = iota((8, NB), 1)
    sub = iota((8, NB), 0)
    own = width // 8
    for step in range(NB // width):
        first = width * step
        top = first // 8
        inside = (lane >= first) & (lane < first + width)
        spread = {}
        for i in range(top, 16):
            for j in range(width):
                if i < top + own and 8 * (i - top) + 7 < j:
                    continue
                spread[i, j] = jnp.broadcast_to(
                    groups[i][:, first + j : first + j + 1], (8, NB)
                )
        diag = {}
        for a in range(width):
            for b in range(a + 1):
                diag[a, b] = jnp.broadcast_to(
                    spread[top + a // 8, b][a % 8 : a % 8 + 1, :], (8, NB)
                )
        rows = []
        for a in range(width):
            row = jnp.broadcast_to(groups[top + a // 8][a % 8 : a % 8 + 1, :], (8, NB))
            rows.append(jnp.where(lane == first + a, 1.0, jnp.where(inside, 0.0, row)))
        recip = {}
        mult = {}
        for j in range(width):
            recip[j] = 1.0 / diag[j, j]
            for a in range(j + 1, width):
                mult[a, j] = diag[a, j] * recip[j]
            for b in range(j + 1, width):
                for a in range(b, width):
                    diag[a, b] = diag[a, b] - mult[a, j] * diag[b, j]
        solved = []
        for a in range(width):
            row = rows[a]
            for b in range(a):
                row = row - mult[a, b] * solved[b]
            solved.append(row)
        for q in range(own):
            total = None
            for s in range(8):
                a = 8 * q + s
                value = solved[a] * lax.rsqrt(diag[a, a])
                total = value if total is None else jnp.where(sub == s, value, total)
            groups[top + q] = total
        back = [None] * width
        for a in reversed(range(width)):
            row = solved[a] * recip[a]
            for b in reversed(range(a + 1, width)):
                row = row - mult[b, a] * back[b]
            back[a] = row
        for i in range(top + own, 16):
            row = jnp.where(inside, 0.0, groups[i])
            for b in reversed(range(width)):
                row = row - spread[i, b] * back[b]
            groups[i] = row
    return groups


def dot3_cat(ah, al, both):
    wide = dot_nt(ah, both)
    return wide[:, :NB] + (wide[:, NB:] + dot_nt(al, both[:NB, :]))


def factor_half(m, lh, ll, xcat, start, origin, blocks, active):
    lower = iota((NB, NB), 0) >= iota((NB, NB), 1)
    eye = iota((NB, NB), 0) == iota((NB, NB), 1)
    base = start * NB

    def solve(k, r, count):
        lo = k * NB
        rows = slice(r * NB, (r + count) * NB)
        ch, cl = split(m[rows, lo : lo + NB])
        part = dot3_cat(ch, cl, xcat[origin + k - start])
        if r == k:
            part = jnp.where(lower, part, 0.0)
        m[rows, lo : lo + NB] = part
        ph, plow = split(part)
        lh[rows, lo : lo + NB] = ph
        ll[rows, lo : lo + NB] = plow

    def update(k, r, count):
        nxt = k * NB + NB
        cols = slice(base, nxt)
        rows = slice(r * NB, (r + count) * NB)
        both = jnp.concatenate([lh[nxt : nxt + NB, cols], ll[nxt : nxt + NB, cols]], axis=0)
        change = dot3_cat(lh[rows, cols], ll[rows, cols], both)
        m[rows, nxt : nxt + NB] = m[rows, nxt : nxt + NB] - change

    def bulk(k):
        for r in range(k + 2, blocks, 2):
            solve(k, r, min(2, blocks - r))
        if k + 1 < start + 4:
            for r in range(k + 2, blocks, 2):
                update(k, r, min(2, blocks - r))

    def store(k, i, value):
        high, low = split(value)
        count = value.shape[0]
        xcat[origin + k - start, 8 * i : 8 * i + count, :] = high
        xcat[origin + k - start, NB + 8 * i : NB + 8 * i + count, :] = low

    def invert(k, work):
        where = slice(k * NB, k * NB + NB)
        busy = active(k)

        @pl.when(busy)
        def _():
            groups = inverse_factor(m[where, where], 8)
            lane = iota((8, NB), 1)
            for i in range(0, 16, 2):
                pair = [
                    jnp.where(lane <= iota((8, NB), 0) + 8 * j, groups[j], 0.0) for j in (i, i + 1)
                ]
                store(k, i, jnp.concatenate(pair, axis=0))
            work()

        @pl.when(jnp.logical_not(busy))
        def _():
            store(k, 0, jnp.where(eye, lax.rsqrt(m[where, where]), 0.0))
            work()

    invert(start, lambda: None)
    for k in range(start, start + 4):
        solve(k, k, 1)
        if k + 1 < blocks:
            solve(k, k + 1, 1)
        if k + 1 < start + 4:
            update(k, k + 1, 1)
            invert(k + 1, functools.partial(bulk, k))
        else:
            bulk(k)


def subtract_square(m, lh, ll, row0, rows, col0, cols, left):
    wide = 2 * NB
    for c in range(col0, col0 + cols, wide):
        for r in range(max(row0, c), row0 + rows, wide):
            change = dot3(
                lh[r : r + wide, left], ll[r : r + wide, left], lh[c : c + wide, left], ll[c : c + wide, left]
            )
            m[r : r + wide, c : c + wide] = m[r : r + wide, c : c + wide] - change


def prepare_kernel(meta, front, shift, first_out, second_out):
    g = meta.g
    eye = (iota((NB, NB), 0) == iota((NB, NB), 1)).astype(f32)

    def alive(block):
        return meta.live(block).astype(f32)

    def column(first, col):
        return front[pl.ds(pl.multiple_of(first * 2, 8) + col, NB, stride=2), :]

    def sym(out, base, col, start):
        here = alive(start + g)
        for s in range(5):
            r = (g + s) % PB
            block = column((start + r) * NB, col)
            block = block * (here * alive(start + r))
            if s == 0:
                block = block + eye * (1.0 - here)

            @pl.when(r >= g)
            def _():
                count = NB if s < 4 else HALF_BLOCK
                out[base + s * NB : base + s * NB + count, :] = block[:count, :]

            @pl.when(r < g)
            def _():
                skip = 0 if s < 4 else HALF_BLOCK
                out[base + s * NB : base + (s + 1) * NB - skip, :] = block.T[skip:, :]

    sym(first_out, 0, 0, 0)
    first_out[SYM : SYM + 8, :] = jnp.broadcast_to(shift[0:1, :], (8, NB))
    here = alive(g)
    for r in range(PB):
        second_out[r * NB : r * NB + NB, :] = column(HALF + r * NB, 0) * (here * alive(PB + r))
    sym(second_out, HALF, 1, PB)


OFFSETS = ((0, 0), (0, 3), (0, 1), (0, 2), (1, 0), (1, 3), (1, 1), (1, 2))


def holder_of(meta, k):
    g = meta.g
    dx, dz = OFFSETS[k]
    return (g // 4 ^ dx) * 4 + (g % 4 + dz) % 4


def place_sym(meta, parts, base, target, address):
    for k in range(PB):
        h = holder_of(meta, k)
        for s in range(5):
            r = (h + s) % PB
            row, cols = address(jnp.maximum(r, h), jnp.minimum(r, h))
            count = NB
            if s == 4:
                count = HALF_BLOCK
                row = pl.multiple_of(row + jnp.where(r >= h, 0, HALF_BLOCK), HALF_BLOCK)
            target[pl.ds(row, count), cols] = parts[k][base + s * NB : base + s * NB + count, :]


def child_first_kernel(meta, *refs):
    parts = refs[:PB]
    lh, ll, xcat, column, shifts, rest, m = refs[PB:]
    g = meta.g
    place_sym(
        meta,
        parts,
        0,
        m,
        lambda r, c: (pl.multiple_of(r * NB, NB), pl.ds(pl.multiple_of(c * NB, NB), NB)),
    )
    for k in range(PB):
        shifts[pl.ds(holder_of(meta, k), 1), :] = parts[k][SYM : SYM + 1, :]
    rest[...] = m[QUART:, QUART:]
    lh[...] = jnp.zeros_like(lh)
    ll[...] = jnp.zeros_like(ll)
    factor_half(m, lh, ll, xcat, 0, 0, PB, lambda k: meta.live(k) > 0)

    @pl.when(g < 4)
    def _():
        mine = pl.multiple_of(g * NB, NB)
        for r in range(PB):
            block = m[r * NB : r * NB + NB, pl.ds(mine, NB)]
            column[r * NB : r * NB + NB, :] = jnp.where(r >= g, block, 0.0)


def child_second_kernel(meta, rest, ah, al, lh, ll, xcat, column, m):
    g = meta.g
    m[...] = rest[...]
    wide = 2 * NB
    for c in range(0, QUART, wide):
        for r in range(c, QUART, wide):
            change = dot3(
                ah[QUART + r : QUART + r + wide, :],
                al[QUART + r : QUART + r + wide, :],
                ah[QUART + c : QUART + c + wide, :],
                al[QUART + c : QUART + c + wide, :],
            )
            m[r : r + wide, c : c + wide] = m[r : r + wide, c : c + wide] - change
    lh[...] = jnp.zeros_like(lh)
    ll[...] = jnp.zeros_like(ll)
    factor_half(m, lh, ll, xcat, 0, 0, 4, lambda k: meta.live(4 + k) > 0)

    @pl.when(g >= 4)
    def _():
        mine = pl.multiple_of((g - 4) * NB, NB)
        for r in range(4):
            block = m[r * NB : r * NB + NB, pl.ds(mine, NB)]
            column[r * NB : r * NB + NB, :] = jnp.where(r >= g - 4, block, 0.0)


def solve_quarter(m, bh, bl, lh, ll, xcat, base):
    step = 2 * NB

    def block(k):
        lo = base + k * NB
        for r in range(0, HALF, step):
            ch, cl = split(m[r : r + step, lo : lo + NB])
            part = dot3_cat(ch, cl, xcat[k])
            m[r : r + step, lo : lo + NB] = part
            ph, plow = split(part)
            bh[r : r + step, lo : lo + NB] = ph
            bl[r : r + step, lo : lo + NB] = plow

    def update(first, count):
        left = slice(base + first * NB, base + (first + count) * NB)
        inner = slice(first * NB, (first + count) * NB)
        target = slice((first + count) * NB, (first + 2 * count) * NB)
        out = slice(base + target.start, base + target.stop)
        th = lh[target, inner]
        tl = ll[target, inner]
        for r in range(0, HALF, step):
            rows = slice(r, r + step)
            m[rows, out] = m[rows, out] - dot3(bh[rows, left], bl[rows, left], th, tl)

    block(0)
    update(0, 1)
    block(1)
    update(0, 2)
    block(2)
    update(2, 1)
    block(3)


def child_third_kernel(meta, ah, al, xa, ca, shifts, lh, ll, xb, cb, *refs):
    parts = refs[:PB]
    factor, schur, m, bh, bl = refs[PB:]
    g = meta.g
    for k in range(PB):
        off = pl.multiple_of(holder_of(meta, k) * NB, NB)
        m[:, pl.ds(off, NB)] = parts[k][:HALF, :]
    place_sym(meta, parts, HALF, schur, lambda r, c: (packed(r, c), slice(None)))
    schur[PACKED : PACKED + 8, :] = shifts[...]
    solve_quarter(m, bh, bl, ah, al, xa, 0)
    th = ah[QUART:, :]
    tl = al[QUART:, :]
    for r in range(0, HALF, 2 * NB):
        rows = slice(r, r + 2 * NB)
        m[rows, QUART:] = m[rows, QUART:] - dot3(bh[rows, :QUART], bl[rows, :QUART], th, tl)
    solve_quarter(m, bh, bl, lh, ll, xb, QUART)
    for c in range(0, PB, 2):
        cols = slice(c * NB, (c + 2) * NB)
        for r in range(c, PB, 2):
            rows = slice(r * NB, (r + 2) * NB)
            change = dot3(bh[rows, :], bl[rows, :], bh[cols, :], bl[cols, :])
            for i in range(2):
                for j in range(2):
                    if r + i >= c + j:
                        at = ((r + i) * (r + i + 1) // 2 + c + j) * NB
                        part = change[i * NB : i * NB + NB, j * NB : j * NB + NB]
                        schur[at : at + NB, :] = schur[at : at + NB, :] - part

    @pl.when(g < 4)
    def _():
        factor[:HALF, :] = ca[...]

    @pl.when(g >= 4)
    def _():
        factor[:QUART, :] = jnp.zeros((QUART, NB), f32)
        factor[QUART:HALF, :] = cb[...]

    factor[HALF:, :] = m[:, pl.ds(pl.multiple_of(g * NB, NB), NB)]


def parent_kernel(meta, own, other, out, m, lh, ll, xcat, inverse):
    g = meta.g
    member = meta.member
    slot = member * PB + g
    for side in range(2):
        for q in range(FB):
            inverse[side, q] = -1
        for c in range(PB):
            live = meta.live(PB + c, side)
            dest = meta.dest(c, side)
            inverse[side, dest] = jnp.where(live > 0, c, -1)
    mine = jnp.int32(0)
    for q in range(FB):
        mine = jnp.where(meta.owner(q) == slot, q, mine)
    sides = (own, other)
    eye = iota((NB, NB), 0) == iota((NB, NB), 1)

    def diagonal(block):
        holder = meta.owner(block)
        a = own[pl.ds(PACKED + holder % PB, 1), :]
        b = other[pl.ds(PACKED + holder % PB, 1), :]
        row = jnp.where(holder // PB == member, a, b)
        return jnp.where(eye, jnp.broadcast_to(row, (NB, NB)), 0.0)

    for p in range(PB):
        for q in range(p, FB):
            where = (slice(q * NB, q * NB + NB), slice(p * NB, p * NB + NB))
            m[where] = diagonal(p) if p == q else jnp.zeros((NB, NB), f32)
            for side in range(2):
                ci = inverse[side, q]
                cj = inverse[side, p]

                @pl.when((ci >= 0) & (cj >= 0))
                def _():
                    m[where] = m[where] + sides[side][pl.ds(packed(ci, cj), NB), :]

    lh[...] = jnp.zeros_like(lh)
    ll[...] = jnp.zeros_like(ll)


    def touched(p):
        return (inverse[0, p] >= 0) | (inverse[1, p] >= 0)

    factor_half(m, lh, ll, xcat, 0, 0, FB, touched)
    subtract_square(m, lh, ll, QUART, F - QUART, QUART, QUART, slice(0, QUART))
    factor_half(m, lh, ll, xcat, 4, 4, FB, touched)

    @pl.when(mine < PB)
    def _():
        off = pl.multiple_of(mine * NB, NB)
        for r in range(FB):
            block = m[r * NB : r * NB + NB, pl.ds(off, NB)]
            out[r * NB : r * NB + NB, :] = jnp.where(r >= mine, block, 0.0)

    @pl.when(mine >= PB)
    def _():
        out[:HALF, :] = jnp.zeros((HALF, NB), f32)
        off = pl.multiple_of(mine * NB, NB)
        rh = lh[pl.ds(off, NB), :]
        rl = ll[pl.ds(off, NB), :]
        diag = diagonal(mine)
        for q in range(PB, FB):
            rows = slice(q * NB, q * NB + NB)
            out[rows, :] = jnp.where(mine == q, diag, 0.0) - dot3(
                lh[rows, :], ll[rows, :], rh, rl
            )
            for side in range(2):
                ci = inverse[side, q]
                cj = inverse[side, mine]
                high = jnp.maximum(jnp.maximum(ci, cj), 0)
                at = packed(high, jnp.maximum(jnp.minimum(ci, cj), 0))

                @pl.when((ci >= cj) & (cj >= 0))
                def _():
                    out[rows, :] = out[rows, :] + sides[side][pl.ds(at, NB), :]

                @pl.when((ci >= 0) & (ci < cj))
                def _():
                    out[rows, :] = out[rows, :] + sides[side][pl.ds(at, NB), :].T


VM = pl.BlockSpec(memory_space=pltpu.VMEM)
SM = pl.BlockSpec(memory_space=pltpu.SMEM)


def shape(*dims, dtype=f32):
    return jax.ShapeDtypeStruct(dims, dtype)


def run(kernel, outs, scratch, flops, limit, meta, *args):
    def wrapped(place, live, dest, owner, *refs):
        kernel(Meta(place, live, dest, owner), *refs)

    return pl.pallas_call(
        wrapped,
        out_shape=outs,
        in_specs=[SM] * 4 + [VM] * len(args),
        out_specs=jax.tree.map(lambda _: VM, outs),
        scratch_shapes=scratch,
        compiler_params=pltpu.CompilerParams(vmem_limit_bytes=limit << 20),
        cost_estimate=pl.CostEstimate(flops=flops, bytes_accessed=1 << 22, transcendentals=0),
    )(*meta, *args)


def permute(value, dx, dz):
    pairs = [(x * 4 + z, (x ^ dx) * 4 + (z + dz) % 4) for x in range(2) for z in range(4)]
    return lax.ppermute(value, "grid", pairs)


def near(value):
    return [value] + [permute(value, 0, 1), permute(value, 0, 3), permute(value, 0, 2), permute(value, 1, 0)]


def far(parts):
    third, side = parts[3], parts[4]
    return parts + [permute(side, 0, 1), permute(side, 0, 3), permute(third, 1, 0)]


def body(child_front, child_live, child_map, parent_owner, parent_shift):
    g = lax.axis_index("grid").astype(jnp.int32)
    leaf = lax.axis_index("leaf").astype(jnp.int32)
    meta = (jnp.stack([g, leaf]), child_live, child_map, parent_owner)
    front = child_front.reshape(2 * F, NB)
    shift = parent_shift.reshape(1, NB)
    first, second = run(
        prepare_kernel,
        (shape(SYM + 8, NB), shape(HALF + SYM, NB)),
        [],
        1 << 20,
        8,
        meta,
        front,
        shift,
    )
    first_parts = far(near(first))
    first_parts, second = lax.optimization_barrier((first_parts, second))
    second_near = near(second)
    ah, al, xa, ca, shifts, rest = run(
        child_first_kernel,
        (
            shape(HALF, QUART, dtype=bf16),
            shape(HALF, QUART, dtype=bf16),
            shape(4, 2 * NB, NB, dtype=bf16),
            shape(HALF, NB),
            shape(8, NB),
            shape(QUART, QUART),
        ),
        [pltpu.VMEM((HALF, HALF), f32)],
        20 * 10**9,
        20,
        meta,
        *first_parts,
    )
    second_near, rest = lax.optimization_barrier((second_near, rest))
    second_parts = far(second_near)
    lh, ll, xb, cb = run(
        child_second_kernel,
        (
            shape(QUART, QUART, dtype=bf16),
            shape(QUART, QUART, dtype=bf16),
            shape(4, 2 * NB, NB, dtype=bf16),
            shape(QUART, NB),
        ),
        [pltpu.VMEM((QUART, QUART), f32)],
        20 * 10**9,
        16,
        meta,
        rest,
        ah,
        al,
    )
    factor, schur = run(
        child_third_kernel,
        (shape(F, NB), shape(PACKED + 8, NB)),
        [
            pltpu.VMEM((HALF, HALF), f32),
            pltpu.VMEM((HALF, HALF), bf16),
            pltpu.VMEM((HALF, HALF), bf16),
        ],
        10**10,
        32,
        meta,
        ah,
        al,
        xa,
        ca,
        shifts,
        lh,
        ll,
        xb,
        cb,
        *second_parts,
    )
    other = lax.ppermute(schur, "leaf", [(s, s ^ 1) for s in range(lax.axis_size("leaf"))])
    done = run(
        parent_kernel,
        shape(F, NB),
        [
            pltpu.VMEM((F, HALF), f32),
            pltpu.VMEM((F, HALF), bf16),
            pltpu.VMEM((F, HALF), bf16),
            pltpu.VMEM((PB, 2 * NB, NB), bf16),
            pltpu.SMEM((2, FB), jnp.int32),
        ],
        40 * 10**9,
        36,
        meta,
        schur,
        other,
    )
    return factor.reshape(1, 1, F, 1, 1, NB), done.reshape(1, 1, F, 1, 1, NB)


def solution(mesh):
    in_specs = (
        P("leaf", None, None, None, "grid", None),
        P(),
        P(),
        P(),
        P("leaf", None, None, "grid", None),
    )
    out_specs = (
        P("leaf", None, None, None, "grid", None),
        P("leaf", None, None, None, "grid", None),
    )
    return jax.shard_map(body, mesh=mesh, in_specs=in_specs, out_specs=out_specs, check_vma=False)
```

```python
import functools

import jax
import jax.numpy as jnp
from jax import lax
from jax.experimental import pallas as pl
from jax.experimental.pallas import tpu as pltpu
from jax.sharding import PartitionSpec as P

NB = 128
PB = 8
FB = 16
HALF = PB * NB
QUART = HALF // 2
F = FB * NB
f32 = jnp.float32
bf16 = jnp.bfloat16


HALF_BLOCK = NB // 2
SYM = 4 * NB + HALF_BLOCK
PACKED = PB * (PB + 1) // 2 * NB


class Meta:
    def __init__(self, place, live, dest, owner):
        self.g = place[0]
        self.leaf = place[1]
        self.member = place[1] % 2
        self.live_table = live
        self.dest_table = dest
        self.owner_table = owner

    def live(self, block, side=0):
        return self.live_table[self.leaf ^ side, 0, block]

    def dest(self, block, side):
        return self.dest_table[self.leaf ^ side, 0, block]

    def owner(self, block):
        return self.owner_table[self.leaf // 2, block]


def packed(row, col):
    return pl.multiple_of((row * (row + 1) // 2 + col) * NB, NB)


def iota(shape, axis):
    return lax.broadcasted_iota(jnp.int32, shape, axis)


def split(x):
    high = x.astype(bf16)
    return high, (x - high.astype(f32)).astype(bf16)


def dot_nt(a, b):
    return lax.dot_general(a, b, (((1,), (1,)), ((), ())), preferred_element_type=f32)


def dot3(ah, al, bh, bl):
    return dot_nt(ah, bh) + (dot_nt(ah, bl) + dot_nt(al, bh))


def inverse_factor(block, width):
    groups = [block[8 * i : 8 * i + 8, :] for i in range(16)]
    lane = iota((8, NB), 1)
    sub = iota((8, NB), 0)
    own = width // 8
    for step in range(NB // width):
        first = width * step
        top = first // 8
        inside = (lane >= first) & (lane < first + width)
        spread = {}
        for i in range(top, 16):
            for j in range(width):
                if i < top + own and 8 * (i - top) + 7 < j:
                    continue
                spread[i, j] = jnp.broadcast_to(
                    groups[i][:, first + j : first + j + 1], (8, NB)
                )
        diag = {}
        for a in range(width):
            for b in range(a + 1):
                diag[a, b] = jnp.broadcast_to(
                    spread[top + a // 8, b][a % 8 : a % 8 + 1, :], (8, NB)
                )
        rows = []
        for a in range(width):
            row = jnp.broadcast_to(groups[top + a // 8][a % 8 : a % 8 + 1, :], (8, NB))
            rows.append(jnp.where(lane == first + a, 1.0, jnp.where(inside, 0.0, row)))
        recip = {}
        mult = {}
        for j in range(width):
            recip[j] = 1.0 / diag[j, j]
            for a in range(j + 1, width):
                mult[a, j] = diag[a, j] * recip[j]
            for b in range(j + 1, width):
                for a in range(b, width):
                    diag[a, b] = diag[a, b] - mult[a, j] * diag[b, j]
        solved = []
        for a in range(width):
            row = rows[a]
            for b in range(a):
                row = row - mult[a, b] * solved[b]
            solved.append(row)
        for q in range(own):
            total = None
            for s in range(8):
                a = 8 * q + s
                value = solved[a] * lax.rsqrt(diag[a, a])
                total = value if total is None else jnp.where(sub == s, value, total)
            groups[top + q] = total
        back = [None] * width
        for a in reversed(range(width)):
            row = solved[a] * recip[a]
            for b in reversed(range(a + 1, width)):
                row = row - mult[b, a] * back[b]
            back[a] = row
        for i in range(top + own, 16):
            row = jnp.where(inside, 0.0, groups[i])
            for b in reversed(range(width)):
                row = row - spread[i, b] * back[b]
            groups[i] = row
    return groups


def dot3_cat(ah, al, both):
    wide = dot_nt(ah, both)
    return wide[:, :NB] + (wide[:, NB:] + dot_nt(al, both[:NB, :]))


def factor_half(m, lh, ll, xcat, start, origin, blocks, active):
    lower = iota((NB, NB), 0) >= iota((NB, NB), 1)
    eye = iota((NB, NB), 0) == iota((NB, NB), 1)
    base = start * NB

    def solve(k, r, count):
        lo = k * NB
        rows = slice(r * NB, (r + count) * NB)
        ch, cl = split(m[rows, lo : lo + NB])
        part = dot3_cat(ch, cl, xcat[origin + k - start])
        if r == k:
            part = jnp.where(lower, part, 0.0)
        m[rows, lo : lo + NB] = part
        ph, plow = split(part)
        lh[rows, lo : lo + NB] = ph
        ll[rows, lo : lo + NB] = plow

    def update(k, r, count):
        nxt = k * NB + NB
        cols = slice(base, nxt)
        rows = slice(r * NB, (r + count) * NB)
        both = jnp.concatenate([lh[nxt : nxt + NB, cols], ll[nxt : nxt + NB, cols]], axis=0)
        change = dot3_cat(lh[rows, cols], ll[rows, cols], both)
        m[rows, nxt : nxt + NB] = m[rows, nxt : nxt + NB] - change

    def bulk(k):
        for r in range(k + 2, blocks, 2):
            solve(k, r, min(2, blocks - r))
        if k + 1 < start + 4:
            for r in range(k + 2, blocks, 2):
                update(k, r, min(2, blocks - r))

    def store(k, i, value):
        high, low = split(value)
        count = value.shape[0]
        xcat[origin + k - start, 8 * i : 8 * i + count, :] = high
        xcat[origin + k - start, NB + 8 * i : NB + 8 * i + count, :] = low

    def invert(k, work):
        where = slice(k * NB, k * NB + NB)
        busy = active(k)

        @pl.when(busy)
        def _():
            groups = inverse_factor(m[where, where], 8)
            lane = iota((8, NB), 1)
            for i in range(0, 16, 2):
                pair = [
                    jnp.where(lane <= iota((8, NB), 0) + 8 * j, groups[j], 0.0) for j in (i, i + 1)
                ]
                store(k, i, jnp.concatenate(pair, axis=0))
            work()

        @pl.when(jnp.logical_not(busy))
        def _():
            store(k, 0, jnp.where(eye, lax.rsqrt(m[where, where]), 0.0))
            work()

    invert(start, lambda: None)
    for k in range(start, start + 4):
        solve(k, k, 1)
        if k + 1 < blocks:
            solve(k, k + 1, 1)
        if k + 1 < start + 4:
            update(k, k + 1, 1)
            invert(k + 1, functools.partial(bulk, k))
        else:
            bulk(k)


def subtract_square(m, lh, ll, row0, rows, col0, cols, left):
    wide = 2 * NB
    for c in range(col0, col0 + cols, wide):
        for r in range(max(row0, c), row0 + rows, wide):
            change = dot3(
                lh[r : r + wide, left], ll[r : r + wide, left], lh[c : c + wide, left], ll[c : c + wide, left]
            )
            m[r : r + wide, c : c + wide] = m[r : r + wide, c : c + wide] - change


def prepare_kernel(meta, front, shift, first_out, second_out):
    g = meta.g
    eye = (iota((NB, NB), 0) == iota((NB, NB), 1)).astype(f32)

    def alive(block):
        return meta.live(block).astype(f32)

    def column(first, col):
        return front[pl.ds(pl.multiple_of(first * 2, 8) + col, NB, stride=2), :]

    def sym(out, base, col, start):
        here = alive(start + g)
        for s in range(5):
            r = (g + s) % PB
            block = column((start + r) * NB, col)
            block = block * (here * alive(start + r))
            if s == 0:
                block = block + eye * (1.0 - here)

            @pl.when(r >= g)
            def _():
                count = NB if s < 4 else HALF_BLOCK
                out[base + s * NB : base + s * NB + count, :] = block[:count, :]

            @pl.when(r < g)
            def _():
                skip = 0 if s < 4 else HALF_BLOCK
                out[base + s * NB : base + (s + 1) * NB - skip, :] = block.T[skip:, :]

    sym(first_out, 0, 0, 0)
    first_out[SYM : SYM + 8, :] = jnp.broadcast_to(shift[0:1, :], (8, NB))
    here = alive(g)
    for r in range(PB):
        second_out[r * NB : r * NB + NB, :] = column(HALF + r * NB, 0) * (here * alive(PB + r))
    sym(second_out, HALF, 1, PB)


OFFSETS = ((0, 0), (0, 3), (0, 1), (0, 2), (1, 0), (1, 3), (1, 1), (1, 2))


def holder_of(meta, k):
    g = meta.g
    dx, dz = OFFSETS[k]
    return (g // 4 ^ dx) * 4 + (g % 4 + dz) % 4


def place_sym(meta, parts, base, target, address):
    for k in range(PB):
        h = holder_of(meta, k)
        for s in range(5):
            r = (h + s) % PB
            row, cols = address(jnp.maximum(r, h), jnp.minimum(r, h))
            count = NB
            if s == 4:
                count = HALF_BLOCK
                row = pl.multiple_of(row + jnp.where(r >= h, 0, HALF_BLOCK), HALF_BLOCK)
            target[pl.ds(row, count), cols] = parts[k][base + s * NB : base + s * NB + count, :]


def child_first_kernel(meta, *refs):
    parts = refs[:PB]
    lh, ll, xcat, column, shifts, rest, m = refs[PB:]
    g = meta.g
    place_sym(
        meta,
        parts,
        0,
        m,
        lambda r, c: (pl.multiple_of(r * NB, NB), pl.ds(pl.multiple_of(c * NB, NB), NB)),
    )
    for k in range(PB):
        shifts[pl.ds(holder_of(meta, k), 1), :] = parts[k][SYM : SYM + 1, :]
    rest[...] = m[QUART:, QUART:]
    lh[...] = jnp.zeros_like(lh)
    ll[...] = jnp.zeros_like(ll)
    factor_half(m, lh, ll, xcat, 0, 0, PB, lambda k: meta.live(k) > 0)

    @pl.when(g < 4)
    def _():
        mine = pl.multiple_of(g * NB, NB)
        for r in range(PB):
            block = m[r * NB : r * NB + NB, pl.ds(mine, NB)]
            column[r * NB : r * NB + NB, :] = jnp.where(r >= g, block, 0.0)


def child_second_kernel(meta, rest, ah, al, lh, ll, xcat, column, m):
    g = meta.g
    m[...] = rest[...]
    wide = 2 * NB
    for c in range(0, QUART, wide):
        for r in range(c, QUART, wide):
            change = dot3(
                ah[QUART + r : QUART + r + wide, :],
                al[QUART + r : QUART + r + wide, :],
                ah[QUART + c : QUART + c + wide, :],
                al[QUART + c : QUART + c + wide, :],
            )
            m[r : r + wide, c : c + wide] = m[r : r + wide, c : c + wide] - change
    lh[...] = jnp.zeros_like(lh)
    ll[...] = jnp.zeros_like(ll)
    factor_half(m, lh, ll, xcat, 0, 0, 4, lambda k: meta.live(4 + k) > 0)

    @pl.when(g >= 4)
    def _():
        mine = pl.multiple_of((g - 4) * NB, NB)
        for r in range(4):
            block = m[r * NB : r * NB + NB, pl.ds(mine, NB)]
            column[r * NB : r * NB + NB, :] = jnp.where(r >= g - 4, block, 0.0)


def solve_quarter(m, bh, bl, lh, ll, xcat, base):
    step = 2 * NB

    def block(k):
        lo = base + k * NB
        for r in range(0, HALF, step):
            ch, cl = split(m[r : r + step, lo : lo + NB])
            part = dot3_cat(ch, cl, xcat[k])
            m[r : r + step, lo : lo + NB] = part
            ph, plow = split(part)
            bh[r : r + step, lo : lo + NB] = ph
            bl[r : r + step, lo : lo + NB] = plow

    def update(first, count):
        left = slice(base + first * NB, base + (first + count) * NB)
        inner = slice(first * NB, (first + count) * NB)
        target = slice((first + count) * NB, (first + 2 * count) * NB)
        out = slice(base + target.start, base + target.stop)
        th = lh[target, inner]
        tl = ll[target, inner]
        for r in range(0, HALF, step):
            rows = slice(r, r + step)
            m[rows, out] = m[rows, out] - dot3(bh[rows, left], bl[rows, left], th, tl)

    block(0)
    update(0, 1)
    block(1)
    update(0, 2)
    block(2)
    update(2, 1)
    block(3)


def child_third_kernel(meta, ah, al, xa, ca, shifts, lh, ll, xb, cb, *refs):
    parts = refs[:PB]
    factor, schur, m, bh, bl = refs[PB:]
    g = meta.g
    for k in range(PB):
        off = pl.multiple_of(holder_of(meta, k) * NB, NB)
        m[:, pl.ds(off, NB)] = parts[k][:HALF, :]
    place_sym(meta, parts, HALF, schur, lambda r, c: (packed(r, c), slice(None)))
    schur[PACKED : PACKED + 8, :] = shifts[...]
    solve_quarter(m, bh, bl, ah, al, xa, 0)
    th = ah[QUART:, :]
    tl = al[QUART:, :]
    for r in range(0, HALF, 2 * NB):
        rows = slice(r, r + 2 * NB)
        m[rows, QUART:] = m[rows, QUART:] - dot3(bh[rows, :QUART], bl[rows, :QUART], th, tl)
    solve_quarter(m, bh, bl, lh, ll, xb, QUART)
    for c in range(0, PB, 2):
        cols = slice(c * NB, (c + 2) * NB)
        for r in range(c, PB, 2):
            rows = slice(r * NB, (r + 2) * NB)
            change = dot3(bh[rows, :], bl[rows, :], bh[cols, :], bl[cols, :])
            for i in range(2):
                for j in range(2):
                    if r + i >= c + j:
                        at = ((r + i) * (r + i + 1) // 2 + c + j) * NB
                        part = change[i * NB : i * NB + NB, j * NB : j * NB + NB]
                        schur[at : at + NB, :] = schur[at : at + NB, :] - part

    @pl.when(g < 4)
    def _():
        factor[:HALF, :] = ca[...]

    @pl.when(g >= 4)
    def _():
        factor[:QUART, :] = jnp.zeros((QUART, NB), f32)
        factor[QUART:HALF, :] = cb[...]

    factor[HALF:, :] = m[:, pl.ds(pl.multiple_of(g * NB, NB), NB)]


def parent_kernel(meta, own, other, out, m, lh, ll, xcat, inverse):
    g = meta.g
    member = meta.member
    slot = member * PB + g
    for side in range(2):
        for q in range(FB):
            inverse[side, q] = -1
        for c in range(PB):
            live = meta.live(PB + c, side)
            dest = meta.dest(c, side)
            inverse[side, dest] = jnp.where(live > 0, c, -1)
    mine = jnp.int32(0)
    for q in range(FB):
        mine = jnp.where(meta.owner(q) == slot, q, mine)
    sides = (own, other)
    eye = iota((NB, NB), 0) == iota((NB, NB), 1)

    def diagonal(block):
        holder = meta.owner(block)
        a = own[pl.ds(PACKED + holder % PB, 1), :]
        b = other[pl.ds(PACKED + holder % PB, 1), :]
        row = jnp.where(holder // PB == member, a, b)
        return jnp.where(eye, jnp.broadcast_to(row, (NB, NB)), 0.0)

    for p in range(PB):
        for q in range(p, FB):
            where = (slice(q * NB, q * NB + NB), slice(p * NB, p * NB + NB))
            m[where] = diagonal(p) if p == q else jnp.zeros((NB, NB), f32)
            for side in range(2):
                ci = inverse[side, q]
                cj = inverse[side, p]

                @pl.when((ci >= 0) & (cj >= 0))
                def _():
                    m[where] = m[where] + sides[side][pl.ds(packed(ci, cj), NB), :]

    lh[...] = jnp.zeros_like(lh)
    ll[...] = jnp.zeros_like(ll)


    def touched(p):
        return (inverse[0, p] >= 0) | (inverse[1, p] >= 0)

    factor_half(m, lh, ll, xcat, 0, 0, FB, touched)
    subtract_square(m, lh, ll, QUART, F - QUART, QUART, QUART, slice(0, QUART))
    factor_half(m, lh, ll, xcat, 4, 4, FB, touched)

    @pl.when(mine < PB)
    def _():
        off = pl.multiple_of(mine * NB, NB)
        for r in range(FB):
            block = m[r * NB : r * NB + NB, pl.ds(off, NB)]
            out[r * NB : r * NB + NB, :] = jnp.where(r >= mine, block, 0.0)

    @pl.when(mine >= PB)
    def _():
        out[:HALF, :] = jnp.zeros((HALF, NB), f32)
        off = pl.multiple_of(mine * NB, NB)
        rh = lh[pl.ds(off, NB), :]
        rl = ll[pl.ds(off, NB), :]
        diag = diagonal(mine)
        for q in range(PB, FB):
            rows = slice(q * NB, q * NB + NB)
            out[rows, :] = jnp.where(mine == q, diag, 0.0) - dot3(
                lh[rows, :], ll[rows, :], rh, rl
            )
            for side in range(2):
                ci = inverse[side, q]
                cj = inverse[side, mine]
                high = jnp.maximum(jnp.maximum(ci, cj), 0)
                at = packed(high, jnp.maximum(jnp.minimum(ci, cj), 0))

                @pl.when((ci >= cj) & (cj >= 0))
                def _():
                    out[rows, :] = out[rows, :] + sides[side][pl.ds(at, NB), :]

                @pl.when((ci >= 0) & (ci < cj))
                def _():
                    out[rows, :] = out[rows, :] + sides[side][pl.ds(at, NB), :].T


VM = pl.BlockSpec(memory_space=pltpu.VMEM)
SM = pl.BlockSpec(memory_space=pltpu.SMEM)


def shape(*dims, dtype=f32):
    return jax.ShapeDtypeStruct(dims, dtype)


def run(kernel, outs, scratch, flops, limit, meta, *args):
    def wrapped(place, live, dest, owner, *refs):
        kernel(Meta(place, live, dest, owner), *refs)

    return pl.pallas_call(
        wrapped,
        out_shape=outs,
        in_specs=[SM] * 4 + [VM] * len(args),
        out_specs=jax.tree.map(lambda _: VM, outs),
        scratch_shapes=scratch,
        compiler_params=pltpu.CompilerParams(vmem_limit_bytes=limit << 20),
        cost_estimate=pl.CostEstimate(flops=flops, bytes_accessed=1 << 22, transcendentals=0),
    )(*meta, *args)


def permute(value, dx, dz):
    pairs = [(x * 4 + z, (x ^ dx) * 4 + (z + dz) % 4) for x in range(2) for z in range(4)]
    return lax.ppermute(value, "grid", pairs)


def near(value):
    return [value] + [permute(value, 0, 1), permute(value, 0, 3), permute(value, 0, 2), permute(value, 1, 0)]


def far(parts):
    third, side = parts[3], parts[4]
    return parts + [permute(side, 0, 1), permute(side, 0, 3), permute(third, 1, 0)]


def body(child_front, child_live, child_map, parent_owner, parent_shift):
    g = lax.axis_index("grid").astype(jnp.int32)
    leaf = lax.axis_index("leaf").astype(jnp.int32)
    meta = (jnp.stack([g, leaf]), child_live, child_map, parent_owner)
    front = child_front.reshape(2 * F, NB)
    shift = parent_shift.reshape(1, NB)
    first, second = run(
        prepare_kernel,
        (shape(SYM + 8, NB), shape(HALF + SYM, NB)),
        [],
        1 << 20,
        8,
        meta,
        front,
        shift,
    )
    first_near, second = lax.optimization_barrier((near(first), second))
    first_parts = far(first_near)
    second_near = near(second)
    ah, al, xa, ca, shifts, rest = run(
        child_first_kernel,
        (
            shape(HALF, QUART, dtype=bf16),
            shape(HALF, QUART, dtype=bf16),
            shape(4, 2 * NB, NB, dtype=bf16),
            shape(HALF, NB),
            shape(8, NB),
            shape(QUART, QUART),
        ),
        [pltpu.VMEM((HALF, HALF), f32)],
        20 * 10**9,
        20,
        meta,
        *first_parts,
    )
    second_near, rest = lax.optimization_barrier((second_near, rest))
    second_parts = far(second_near)
    lh, ll, xb, cb = run(
        child_second_kernel,
        (
            shape(QUART, QUART, dtype=bf16),
            shape(QUART, QUART, dtype=bf16),
            shape(4, 2 * NB, NB, dtype=bf16),
            shape(QUART, NB),
        ),
        [pltpu.VMEM((QUART, QUART), f32)],
        20 * 10**9,
        16,
        meta,
        rest,
        ah,
        al,
    )
    factor, schur = run(
        child_third_kernel,
        (shape(F, NB), shape(PACKED + 8, NB)),
        [
            pltpu.VMEM((HALF, HALF), f32),
            pltpu.VMEM((HALF, HALF), bf16),
            pltpu.VMEM((HALF, HALF), bf16),
        ],
        10**10,
        32,
        meta,
        ah,
        al,
        xa,
        ca,
        shifts,
        lh,
        ll,
        xb,
        cb,
        *second_parts,
    )
    other = lax.ppermute(schur, "leaf", [(s, s ^ 1) for s in range(lax.axis_size("leaf"))])
    done = run(
        parent_kernel,
        shape(F, NB),
        [
            pltpu.VMEM((F, HALF), f32),
            pltpu.VMEM((F, HALF), bf16),
            pltpu.VMEM((F, HALF), bf16),
            pltpu.VMEM((PB, 2 * NB, NB), bf16),
            pltpu.SMEM((2, FB), jnp.int32),
        ],
        40 * 10**9,
        36,
        meta,
        schur,
        other,
    )
    return factor.reshape(1, 1, F, 1, 1, NB), done.reshape(1, 1, F, 1, 1, NB)


def solution(mesh):
    in_specs = (
        P("leaf", None, None, None, "grid", None),
        P(),
        P(),
        P(),
        P("leaf", None, None, "grid", None),
    )
    out_specs = (
        P("leaf", None, None, None, "grid", None),
        P("leaf", None, None, None, "grid", None),
    )
    return jax.shard_map(body, mesh=mesh, in_specs=in_specs, out_specs=out_specs, check_vma=False)
```
